128 devices in a mesh: span: 8 (over z, y_hi), slab: 16 (over y_lo, x, core).
Axes of the slice: x: 4, y: 4 (y_hi: 2, y_lo: 2; y = y_hi * 2 + y_lo), z: 4, core: 2. Of those that a mesh axis runs over, the one named last changes fastest.
Arguments:
- activations: bfloat16 [32, 128, 128, 128], P('span', 'slab'), may hold values from -24 to 24
- cotangent: bfloat16 [32, 128, 128, 128], P('span', 'slab'), may hold values from -6 to 6
- conv_weight: bfloat16 [3, 3, 3, 128, 128], replicated, may hold values from -0.109375 to 0.109375
- norm_gain: float32 [128], replicated, may hold values from 0.25 to 1.75
- norm_shift: float32 [128], replicated, may hold values from -3 to 3
Outputs:
- input_grad: bfloat16 [32, 128, 128, 128], P('span', 'slab')
- weight_grad: float32 [3, 3, 3, 128, 128], replicated
- gain_grad: float32 [128], replicated
- shift_grad: float32 [128], replicated
- bias_grad: float32 [128], replicated
The draws below stay inside these ranges and needn't reach their ends.
All inputs are finite; a program needn't handle non-finite values.
Results may differ from the reference program's by a relative error of at most 0.0029.
Values may be sent and summed in bfloat16 or wider, within the bound.
A program may use at most 128 MiB of HBM per device.

```python
import jax
import jax.numpy as jnp
from jax import lax

C = 128
G = 32
WIDTH = 128
NT = 32
NH = 128


def draw_activations(key, part):
    base_key = jax.random.fold_in(key, 7)
    key_main = jax.random.fold_in(base_key, 0)
    frame_pos = jnp.arange(NT, dtype=jnp.float32) / max(NT - 1, 1)
    row_pos = jnp.arange(NH, dtype=jnp.float32) / max(NH - 1, 1)
    ramp = (1.0 + 0.75 * frame_pos)[:, None, None, None] * (1.0 + 0.75 * row_pos)[None, :, None, None]
    base = jax.random.truncated_normal(key_main, -4.0, 4.0, (NT, NH, WIDTH, C), jnp.float32)
    return (base * ramp).astype(jnp.bfloat16)


def levels(key, dims, cuts, least, top_value):
    def one(position, parts):
        draws = jax.random.uniform(jax.random.fold_in(jax.random.fold_in(key, 6), position), (parts,), jnp.float32, least / len(cuts), top_value / len(cuts))
        return jnp.repeat(jnp.exp(draws), dims[position] // parts).reshape((-1,) + (1,) * (len(dims) - position - 1))

    factor_of = one(*cuts[0])
    for cut in cuts[1:]:
        factor_of = factor_of * one(*cut)
    return factor_of


def scatter_about(key, extent, spread, reach, cuts=(), held_as=jnp.bfloat16):
    drawn = spread * jax.random.normal(key, extent, jnp.float32)
    if cuts:
        drawn = drawn * levels(key, extent, cuts, -0.22, 0.18)
    return jnp.clip(drawn, -reach, reach).astype(held_as)


def setup_inputs(seed: int = 0) -> dict:
    seeds = jax.random.split(jax.random.key(seed), 6)
    activations = draw_activations(jax.random.fold_in(seeds[5], 71), 0)
    cotangent = scatter_about(seeds[1], (NT, NH, WIDTH, C), 1.0, 6.0, ((0, 8), (1, 16)))
    conv_weight = scatter_about(seeds[2], (3, 3, 3, C, C), (27 * C) ** -0.5, 0.109375)
    norm_gain = jnp.clip(1.0 + 0.15 * jax.random.normal(seeds[3], (C,), jnp.float32), 0.25, 1.75)
    norm_shift = scatter_about(seeds[4], (C,), 0.5, 3.0, (), jnp.float32)
    return dict(activations=activations, cotangent=cotangent, conv_weight=conv_weight, norm_gain=norm_gain, norm_shift=norm_shift)


def tap_columns(padded, time_start, row_start, time_count, row_count, col_count, col_starts):
    window = padded[time_start:time_start + time_count, row_start:row_start + row_count]
    pieces = [window[:, :, begin:begin + col_count] for begin in col_starts]
    return jnp.concatenate(pieces, axis=-1).reshape(time_count * row_count * col_count, -1)

def reference(activations, cotangent, conv_weight, norm_gain, norm_shift):
    group_size = C // G
    members = NT * NH * WIDTH * group_size
    inputs = activations.astype(jnp.float32)
    first_sums = lax.optimization_barrier(jnp.sum(inputs, axis=(0, 1, 2)))
    square_sums = lax.optimization_barrier(jnp.sum(inputs * inputs, axis=(0, 1, 2)))
    group_mean = first_sums.reshape(G, group_size).sum(axis=1) / members
    variance = square_sums.reshape(G, group_size).sum(axis=1) / members - group_mean * group_mean
    inv_std = lax.rsqrt(variance + 1e-06)
    inv_chan = jnp.repeat(inv_std, group_size)
    normed = (inputs - jnp.repeat(group_mean, group_size)) * inv_chan
    scaled = normed * norm_gain + norm_shift
    activated = (scaled * jax.nn.sigmoid(scaled)).astype(jnp.bfloat16)
    act_pad = jnp.pad(activated, ((2, 0), (1, 1), (1, 1), (0, 0)))
    grad_pad = jnp.pad(cotangent, ((0, 2), (1, 1), (1, 1), (0, 0)))
    grad_flat = cotangent.reshape(-1, C)
    weight_rows = []
    act_grad = jnp.zeros((NT * NH * WIDTH, C), jnp.float32)
    for tap_time in range(3):
        for tap_row in range(3):
            columns = tap_columns(act_pad, tap_time, tap_row, NT, NH, WIDTH, (0, 1, 2))
            weight_rows.append(lax.dot_general(columns, grad_flat, (((0,), (0,)), ((), ())), preferred_element_type=jnp.float32))
            grad_cols = tap_columns(grad_pad, 2 - tap_time, 2 - tap_row, NT, NH, WIDTH, (2, 1, 0))
            stacked = jnp.concatenate([conv_weight[tap_time, tap_row, tap_col].T for tap_col in range(3)], axis=0)
            act_grad = act_grad + jnp.dot(grad_cols, stacked, preferred_element_type=jnp.float32)
    weight_sum = jnp.concatenate(weight_rows, axis=0).reshape(3, 3, 3, C, C)
    act_grad = act_grad.reshape(NT, NH, WIDTH, C)
    sigma = jax.nn.sigmoid(scaled)
    pre_grad = act_grad * sigma * (1.0 + scaled * (1.0 - sigma))
    gain_sum = lax.optimization_barrier(jnp.sum(pre_grad * normed, axis=(0, 1, 2)))
    shift_sum = lax.optimization_barrier(jnp.sum(pre_grad, axis=(0, 1, 2)))
    bias_sum = lax.optimization_barrier(jnp.sum(cotangent.astype(jnp.float32), axis=(0, 1, 2)))
    mean_one = jnp.repeat((norm_gain * shift_sum).reshape(G, group_size).sum(axis=1) / members, group_size)
    mean_two = jnp.repeat((norm_gain * gain_sum).reshape(G, group_size).sum(axis=1) / members, group_size)
    input_grad = (inv_chan * (norm_gain * pre_grad - mean_one - normed * mean_two)).astype(jnp.bfloat16)
    factor = 1.0 / jnp.sqrt(jnp.float32(NT * NH * WIDTH))
    return (input_grad, weight_sum * factor, gain_sum * factor, shift_sum * factor, bias_sum * factor)
```

```python
import functools

import jax
import jax.numpy as jnp
from jax import lax
from jax.experimental import pallas as pl
from jax.experimental.pallas import tpu as pltpu
from jax.sharding import PartitionSpec as P

MESH = pl.DeviceIdType.MESH
F32 = jnp.float32
BF16 = jnp.bfloat16
NF, NR, W, C = 4, 8, 128, 128
ROWS = NR * W
CELLS = 32 * 128 * 128
MEMBERS = CELLS * 4
SCALE = float(CELLS) ** -0.5
NT_DIMS = (((1,), (1,)), ((), ()))


def group_sum(v):
    lane = lax.broadcasted_iota(jnp.int32, v.shape, 1)
    v = v + jnp.where(lane % 2 == 0, pltpu.roll(v, C - 1, 1), pltpu.roll(v, 1, 1))
    return v + jnp.where(lane % 4 < 2, pltpu.roll(v, C - 2, 1), pltpu.roll(v, 2, 1))


def kernel(
    act_hbm, cot_hbm, w_hbm, gain_ref, shift_ref,
    out_hbm, wout_hbm, sums_ref,
    act_v, grad_v, w_v, at_v, ag_v, dv_v, wacc, rs_core, rs_axis, rs_own, rs_plane, wout, outb, stat, arb, ara,
    loc_sem, out_sem, halo_s, halo_r, arb_s, arb_r, ara_s, ara_r,
    c_s, c_r, x_s, x_r, p_s, p_r, gp_s, gp_r, gx_s, gx_r, gc_s, gc_r,
):
    span, slab = lax.axis_index("span"), lax.axis_index("slab")
    y_lo, xc = slab // 8, slab % 8
    x, core = xc // 2, xc % 2
    plane = span * 2 + y_lo

    def in_plane(q):
        return (q // 2, (q % 2) * 8 + xc)

    def in_row(j):
        return (span, y_lo * 8 + j)

    before, after = (span + 7) % 8, (span + 1) % 8
    above, below = (slab + 15) % 16, (slab + 1) % 16

    copy_act = pltpu.make_async_copy(act_hbm, act_v, loc_sem.at[0])
    copy_cot = pltpu.make_async_copy(cot_hbm, grad_v.at[pl.ds(0, NF), pl.ds(1, NR)], loc_sem.at[1])
    copy_w = pltpu.make_async_copy(w_hbm, w_v, loc_sem.at[2])
    copy_act.start()
    copy_cot.start()
    copy_w.start()

    barrier = pltpu.get_barrier_semaphore()

    def signal(device):
        pl.semaphore_signal(barrier, inc=1, device_id=device, device_id_type=MESH)

    for d in range(1, 16):
        signal(in_plane((plane + d) % 16))
    for d in range(1, 8):
        signal(in_row((xc + d) % 8))
    for device in (
        (span, above), (span, below), (before, above), (before, below), (after, above), (after, below)
    ):
        signal(device)

    def remote(src, dst, send, recv, device):
        return pltpu.make_async_remote_copy(
            src_ref=src, dst_ref=dst, send_sem=send, recv_sem=recv, device_id=device, device_id_type=MESH
        )

    def fold(v):
        return v.reshape(-1, 8, C).sum(axis=0)

    copy_act.wait()

    def local_sums(i, carry):
        one, two = carry
        v = act_v[i // NR, i % NR].astype(F32)
        return one + fold(v), two + fold(v * v)

    zero8 = jnp.zeros((8, C), F32)
    one, two = lax.fori_loop(0, NF * NR, local_sums, (zero8, zero8))
    row = lax.broadcasted_iota(jnp.int32, (8, C), 0)

    def stacked(*sums):
        value = zero8
        for n, v in enumerate(sums):
            value = jnp.where(row == n, jnp.broadcast_to(v.sum(axis=0, keepdims=True), (8, C)), value)
        return value

    def plane_copy(n, peer, slot):
        return remote(stat.at[n, 0], arb.at[n, slot], arb_s.at[n, peer], arb_r.at[n, slot], in_plane(peer))

    def row_copy(n, peer, slot):
        return remote(stat.at[n, 1], ara.at[n, slot], ara_s.at[n, peer], ara_r.at[n, slot], in_row(peer))

    def reduce_start(n, value):
        stat[n, 0] = value
        arb[n, plane] = value
        for d in range(1, 16):
            plane_copy(n, (plane + d) % 16, plane).start()

    def reduce_middle(n):
        for d in range(1, 16):
            plane_copy(n, (plane + d) % 16, (plane + d) % 16).wait_recv()
        value = arb[n].sum(axis=0)
        stat[n, 1] = value
        ara[n, xc] = value
        for d in range(1, 8):
            row_copy(n, (xc + d) % 8, xc).start()

    def reduce_end(n):
        for d in range(1, 8):
            row_copy(n, (xc + d) % 8, (xc + d) % 8).wait_recv()
        return ara[n].sum(axis=0)

    def reduce_drain(n):
        for d in range(1, 16):
            plane_copy(n, (plane + d) % 16, plane).wait_send()
        for d in range(1, 8):
            row_copy(n, (xc + d) % 8, xc).wait_send()

    pl.semaphore_wait(barrier, 28)

    halo = [
        remote(cot_hbm.at[:, 0], grad_v.at[pl.ds(0, NF), NR + 1], halo_s.at[0], halo_r.at[0], (span, above)),
        remote(cot_hbm.at[:, NR - 1], grad_v.at[pl.ds(0, NF), 0], halo_s.at[1], halo_r.at[1], (span, below)),
        remote(cot_hbm.at[0], grad_v.at[NF, pl.ds(1, NR)], halo_s.at[2], halo_r.at[2], (before, slab)),
        remote(cot_hbm.at[pl.ds(0, 2), 0], grad_v.at[pl.ds(NF, 2), NR + 1], halo_s.at[3], halo_r.at[3], (before, above)),
        remote(cot_hbm.at[pl.ds(0, 2), NR - 1], grad_v.at[pl.ds(NF, 2), 0], halo_s.at[4], halo_r.at[4], (before, below)),
        remote(cot_hbm.at[1], grad_v.at[NF + 1, pl.ds(1, NR)], halo_s.at[5], halo_r.at[5], (before, slab)),
    ]
    halo[0].start()
    halo[1].start()
    reduce_start(0, stacked(one, two))
    for h in halo[2:]:
        h.start()

    copy_cot.wait()

    def bias_local(i, carry):
        return carry + fold(grad_v[i // NR, 1 + i % NR].astype(F32))

    bias = lax.fori_loop(0, NF * NR, bias_local, zero8)

    def clear_rows(frames):
        @pl.when(slab == 0)
        def _():
            for f in frames:
                grad_v[f, 0] = jnp.zeros((W, C), BF16)

        @pl.when(slab == 15)
        def _():
            for f in frames:
                grad_v[f, NR + 1] = jnp.zeros((W, C), BF16)

    def shifted_sum(o):
        o = o.reshape(-1, W, 3 * C)
        pixel = lax.broadcasted_iota(jnp.int32, (1, W, C), 1)
        left = pltpu.roll(o[:, :, :C], W - 1, 1)
        right = pltpu.roll(o[:, :, 2 * C :], 1, 1)
        return o[:, :, C : 2 * C] + jnp.where(pixel < W - 1, left, 0.0) + jnp.where(pixel > 0, right, 0.0)

    def act_grad(t, taps, add):
        rhs = jnp.concatenate([w_v[a * 3 + b] for a in taps for b in range(3)], axis=1)
        half = NR // 2

        def part(i, _):
            r = i * half
            lhs = jnp.concatenate(
                [
                    grad_v[t + 2 - a, pl.ds(r + 2 - b, half)].reshape(half * W, C)
                    for a in taps
                    for b in range(3)
                ],
                axis=1,
            )
            o = shifted_sum(lax.dot_general(lhs, rhs, NT_DIMS, preferred_element_type=F32))
            if add:
                o = o + ag_v[t, pl.ds(r, half)]
            ag_v[t, pl.ds(r, half)] = o
            return 0

        lax.fori_loop(0, 2, part, 0)

    copy_w.wait()
    halo[0].wait_recv()
    halo[1].wait_recv()
    clear_rows(range(NF))
    act_grad(0, (2, 1, 0), False)
    reduce_middle(0)
    act_grad(1, (2, 1, 0), False)
    act_grad(2, (2, 1), False)
    act_grad(3, (2,), False)

    sums = group_sum(reduce_end(0))
    mean = sums[0:1] / MEMBERS
    variance = sums[1:2] / MEMBERS - mean * mean
    inv = lax.rsqrt(variance + 1e-06)
    gain, shift = gain_ref[...], shift_ref[...]

    def activate(i, _):
        t, r = i // NR, i % NR
        normed = (act_v[t, r].astype(F32) - mean) * inv
        scaled = normed * gain + shift
        sigma = jax.nn.sigmoid(scaled)
        dv_v[t, r] = sigma * (1.0 + scaled * (1.0 - sigma))
        turned = (scaled * sigma).T
        pixel = lax.broadcasted_iota(jnp.int32, (C, W), 1)
        at_v[t, r, 0:C] = jnp.where(pixel > 0, pltpu.roll(turned, 1, 1), 0.0).astype(BF16)
        at_v[t, r, C : 2 * C] = turned.astype(BF16)
        at_v[t, r, 2 * C : 3 * C] = jnp.where(pixel < W - 1, pltpu.roll(turned, W - 1, 1), 0.0).astype(BF16)
        return 0

    lax.fori_loop(0, NF * NR, activate, 0)

    def weight_part(a, frames, fresh):
        def one_frame(t):
            lhs = jnp.concatenate([at_v[t, r] for r in range(NR)], axis=1)
            rhs = jnp.concatenate(
                [grad_v[t + 2 - a, 2 - b : 2 - b + NR].reshape(ROWS, C) for b in range(3)], axis=1
            )
            return jnp.dot(lhs, rhs, preferred_element_type=F32)

        def put(o, add):
            for b in range(3):
                v = o[:, b * C : (b + 1) * C].reshape(3, C, C)
                if add:
                    v = v + wacc[a, 3 * b : 3 * b + 3]
                wacc[a, 3 * b : 3 * b + 3] = v

        first, last = frames
        if fresh:
            put(one_frame(first), False)
            first += 1

        def step(t, _):
            put(one_frame(t), True)
            return 0

        if first < last:
            lax.fori_loop(first, last, step, 0)

    half0 = core * 64
    mine0 = half0 + x * 16
    twin = in_row(xc + 1 - 2 * core)

    def rows(ref, a, start, size):
        return ref.at[a, :, pl.ds(pl.multiple_of(start, 16), size)]

    def x_peer(k):
        return in_row(k * 2 + core)

    def core_copy(a):
        return remote(rows(wacc, a, 64 - half0, 64), rs_core.at[a], c_s.at[a], c_r.at[a], twin)

    def axis_copy(a, k, slot):
        return remote(
            rows(wacc, a, half0 + k * 16, 16), rs_axis.at[a, slot], x_s.at[a, k], x_r.at[a, slot], x_peer(k)
        )

    def piece_copy(a, p, slot):
        return remote(rs_own.at[a, p], rs_plane.at[a, slot], p_s.at[a, p], p_r.at[a, slot], in_plane(p))

    def tile(a, p):
        return wout.at[a, p, pl.ds(pl.multiple_of(mine0, 16), 16)]

    def tile_copy(a, p, owner):
        return remote(tile(a, owner), tile(a, owner), gp_s.at[a, p], gp_r.at[a, owner], in_plane(p))

    def gather_axis(a, k, owner):
        part = rows(wout, a, half0 + owner * 16, 16)
        return remote(part, part, gx_s.at[a, k], gx_r.at[a, owner], x_peer(k))

    def gather_core(a, start):
        part = rows(wout, a, start, 64)
        return remote(part, part, gc_s.at[a], gc_r.at[a], twin)

    def s0(a):
        core_copy(a).start()

    def s1(a):
        core_copy(a).wait_recv()
        here = pl.ds(pl.multiple_of(half0, 16), 64)
        wacc[a, :, here] = wacc[a, :, here] + rs_core[a]
        for d in range(1, 4):
            axis_copy(a, (x + d) % 4, x).start()

    def s2(a):
        for d in range(1, 4):
            axis_copy(a, (x + d) % 4, (x + d) % 4).wait_recv()
        rs_axis[a, x] = wacc[a, :, pl.ds(pl.multiple_of(mine0, 16), 16)]
        rs_own[a] = rs_axis[a].sum(axis=0)
        for d in range(1, 16):
            p = (plane + d) % 16

            @pl.when(p < 9)
            def _(p=p):
                piece_copy(a, p, plane).start()

    def s3(a):
        @pl.when(plane < 9)
        def _():
            for d in range(1, 16):
                piece_copy(a, plane, (plane + d) % 16).wait_recv()
            rs_plane[a, plane] = rs_own[a, plane]
            total = rs_plane[a].sum(axis=0) * SCALE
            wout[a, plane, pl.ds(pl.multiple_of(mine0, 16), 16)] = total.astype(BF16)
            for d in range(1, 16):
                tile_copy(a, (plane + d) % 16, plane).start()

    def s4(a):
        for p in range(9):

            @pl.when(plane != p)
            def _(p=p):
                tile_copy(a, p, p).wait_recv()

        for d in range(1, 4):
            gather_axis(a, (x + d) % 4, x).start()

    def s5(a):
        for d in range(1, 4):
            gather_axis(a, (x + d) % 4, (x + d) % 4).wait_recv()
        gather_core(a, half0).start()

    def s6(a):
        gather_core(a, 64 - half0).wait_recv()

    def drain(a):
        core_copy(a).wait_send()
        for d in range(1, 4):
            axis_copy(a, (x + d) % 4, x).wait_send()
            gather_axis(a, (x + d) % 4, x).wait_send()
        for d in range(1, 16):
            p = (plane + d) % 16

            @pl.when(p < 9)
            def _(p=p):
                piece_copy(a, p, plane).wait_send()

        @pl.when(plane < 9)
        def _():
            for d in range(1, 16):
                tile_copy(a, (plane + d) % 16, plane).wait_send()

        gather_core(a, half0).wait_send()

    weight_part(2, (0, 4), True)
    s0(2)
    weight_part(1, (0, 3), True)
    s1(2)
    weight_part(0, (0, 2), True)
    s2(2)

    for h in halo[2:]:
        h.wait_recv()
    clear_rows((NF, NF + 1))

    @pl.when(span == 7)
    def _():
        def clear(i, _):
            grad_v[NF + i // (NR + 2), i % (NR + 2)] = jnp.zeros((W, C), BF16)
            return 0

        lax.fori_loop(0, 2 * (NR + 2), clear, 0)

    weight_part(1, (3, 4), False)
    s0(1)
    weight_part(0, (2, 4), False)
    s0(0)
    s1(1)
    s3(2)
    act_grad(2, (0,), True)
    s1(0)
    s2(1)
    act_grad(3, (1, 0), True)
    s2(0)

    def finish(i, carry):
        t, r = i // NR, i % NR
        normed = (act_v[t, r].astype(F32) - mean) * inv
        pre = ag_v[t, r] * dv_v[t, r]
        ag_v[t, r] = pre
        return carry[0] + fold(pre * normed), carry[1] + fold(pre)

    gain_sum, shift_sum = lax.fori_loop(0, NF * NR, finish, (zero8, zero8))
    reduce_start(1, stacked(gain_sum, shift_sum, bias))
    s3(1)
    s4(2)
    s3(0)
    s5(2)
    reduce_middle(1)
    s4(1)
    s4(0)
    total = reduce_end(1)
    sums_ref[...] = total * SCALE
    means = group_sum(total * gain) / MEMBERS
    mean_two, mean_one = means[0:1], means[1:2]

    def result(i, _):
        t, r = i // NR, i % NR
        normed = (act_v[t, r].astype(F32) - mean) * inv
        outb[t, r] = (inv * (gain * ag_v[t, r] - mean_one - normed * mean_two)).astype(BF16)
        return 0

    lax.fori_loop(0, NF * NR, result, 0)
    copy_out = pltpu.make_async_copy(outb, out_hbm, out_sem.at[0])
    copy_out.start()
    s5(1)
    s5(0)
    s6(2)
    s6(1)
    s6(0)
    copy_weights = pltpu.make_async_copy(wout, wout_hbm, out_sem.at[1])
    copy_weights.start()
    for h in halo:
        h.wait_send()
    for n in range(2):
        reduce_drain(n)
    for a in range(3):
        drain(a)
    copy_out.wait()
    copy_weights.wait()


def body(activations, cotangent, conv_weight, norm_gain, norm_shift):
    anywhere = pl.BlockSpec(memory_space=pl.ANY)
    vmem = pl.BlockSpec(memory_space=pltpu.VMEM)
    dma = pltpu.SemaphoreType.DMA
    input_grad, weights, sums = pl.pallas_call(
        kernel,
        out_shape=(
            jax.ShapeDtypeStruct((NF, NR, W, C), BF16),
            jax.ShapeDtypeStruct((3, 9, C, C), BF16),
            jax.ShapeDtypeStruct((8, C), F32),
        ),
        in_specs=[anywhere, anywhere, anywhere, vmem, vmem],
        out_specs=(anywhere, anywhere, vmem),
        scratch_shapes=[
            pltpu.VMEM((NF, NR, W, C), BF16),
            pltpu.VMEM((NF + 2, NR + 2, W, C), BF16),
            pltpu.VMEM((9, 3 * C, C), BF16),
            pltpu.VMEM((NF, NR, 3 * C, W), BF16),
            pltpu.VMEM((NF, NR, W, C), F32),
            pltpu.VMEM((NF, NR, W, C), F32),
            pltpu.VMEM((3, 9, C, C), F32),
            pltpu.VMEM((3, 9, 64, C), F32),
            pltpu.VMEM((3, 4, 9, 16, C), F32),
            pltpu.VMEM((3, 9, 16, C), F32),
            pltpu.VMEM((3, 16, 16, C), F32),
            pltpu.VMEM((3, 9, C, C), BF16),
            pltpu.VMEM((NF, NR, W, C), BF16),
            pltpu.VMEM((2, 2, 8, C), F32),
            pltpu.VMEM((2, 16, 8, C), F32),
            pltpu.VMEM((2, 8, 8, C), F32),
            dma((3,)), dma((2,)), dma((6,)), dma((6,)),
            dma((2, 16)), dma((2, 16)), dma((2, 8)), dma((2, 8)),
            dma((3,)), dma((3,)), dma((3, 4)), dma((3, 4)), dma((3, 9)), dma((3, 16)),
            dma((3, 16)), dma((3, 9)), dma((3, 4)), dma((3, 4)), dma((3,)), dma((3,)),
        ],
        compiler_params=pltpu.CompilerParams(
            collective_id=0, has_side_effects=True, vmem_limit_bytes=56 * 1024 * 1024
        ),
    )(
        activations,
        cotangent,
        conv_weight.reshape(9, 3 * C, C),
        norm_gain.reshape(1, C),
        norm_shift.reshape(1, C),
    )
    weight_grad = weights.astype(F32).reshape(3, 3, 3, C, C)
    return input_grad, weight_grad, sums[0], sums[1], sums[2]


def solution(mesh):
    placed = (P("span", "slab", None, None), P("span", "slab", None, None), P(), P(), P())
    return jax.shard_map(
        body,
        mesh=mesh,
        in_specs=placed,
        out_specs=(P("span", "slab", None, None), P(), P(), P(), P()),
        check_vma=False,
    )
```

```python
import jax
import jax.numpy as jnp
from jax import lax
from jax.experimental import pallas as pl
from jax.experimental.pallas import tpu as pltpu
from jax.sharding import PartitionSpec as P

MESH = pl.DeviceIdType.MESH
F32 = jnp.float32
BF16 = jnp.bfloat16
NF, NR, W, C = 4, 8, 128, 128
ROWS = NR * W
CELLS = 32 * 128 * 128
MEMBERS = CELLS * 4
SCALE = float(CELLS) ** -0.5
NT_DIMS = (((1,), (1,)), ((), ()))


def group_sum(v):
    lane = lax.broadcasted_iota(jnp.int32, v.shape, 1)
    v = v + jnp.where(lane % 2 == 0, pltpu.roll(v, C - 1, 1), pltpu.roll(v, 1, 1))
    return v + jnp.where(lane % 4 < 2, pltpu.roll(v, C - 2, 1), pltpu.roll(v, 2, 1))


def fold(v):
    return v.reshape(-1, 8, C).sum(axis=0)


def kernel(
    act_hbm, cot_hbm, w_hbm, gain_ref, shift_ref,
    out_hbm, wout_hbm, sums_ref,
    act_v, grad_v, w_v, at_v, ag_v, dv_v, wacc, rs_core, rs_axis, rs_own, rs_plane, wout, outb, stat, arb, ara, relay,
    loc_sem, out_sem, halo_s, halo_r, hop_s, hop_r, ar_s, ar_r,
    c_s, c_r, x_s, x_r, p_s, p_r, gp_s, gp_r, gx_s, gx_r, gc_s, gc_r,
):
    span, slab = lax.axis_index("span"), lax.axis_index("slab")
    z, y = span // 2, (span % 2) * 2 + slab // 8
    xc = slab % 8
    x, core = xc // 2, xc % 2

    def chip(cz, cy, cx, cc=core):
        return (cz * 2 + cy // 2, (cy % 2) * 8 + cx * 2 + cc)

    copies_act = [pltpu.make_async_copy(act_hbm.at[t], act_v.at[t], loc_sem.at[t]) for t in range(NF)]
    copy_cot = pltpu.make_async_copy(cot_hbm, grad_v.at[pl.ds(0, NF), pl.ds(1, NR)], loc_sem.at[NF])
    copy_w = pltpu.make_async_copy(w_hbm, w_v, loc_sem.at[NF + 1])
    for copy in copies_act:
        copy.start()
    copy_cot.start()
    copy_w.start()

    barrier = pltpu.get_barrier_semaphore()
    above = (span, (slab + 15) % 16)
    below = (span, (slab + 1) % 16)
    greeted = [above, below]
    for dz in range(4):
        for dy in range(4):
            for dx in range(4):
                if 0 in (dz, dy, dx) and (dz, dy, dx) != (0, 0, 0):
                    greeted.append(chip((z + dz) % 4, (y + dy) % 4, (x + dx) % 4))
    for dx in range(4):
        greeted.append(chip(z, y, (x + dx) % 4, 1 - core))
    for device in greeted:
        pl.semaphore_signal(barrier, inc=1, device_id=device, device_id_type=MESH)

    def remote(src, dst, send, recv, device):
        return pltpu.make_async_remote_copy(
            src_ref=src, dst_ref=dst, send_sem=send, recv_sem=recv, device_id=device, device_id_type=MESH
        )

    def take(ref, recv):
        remote(ref, ref, recv, recv, below).wait_recv()

    def sent(ref, send):
        remote(ref, ref, send, send, below).wait_send()

    zero8 = jnp.zeros((8, C), F32)
    one, two = zero8, zero8
    for t in range(NF):
        copies_act[t].wait()

        def local_sums(r, carry, t=t):
            v = act_v[t, r].astype(F32)
            return carry[0] + fold(v), carry[1] + fold(v * v)

        one, two = lax.fori_loop(0, NR, local_sums, (one, two), unroll=2)
    row = lax.broadcasted_iota(jnp.int32, (8, C), 0)

    def stacked(*sums):
        value = zero8
        for n, v in enumerate(sums):
            value = jnp.where(row == n, jnp.broadcast_to(v.sum(axis=0, keepdims=True), (8, C)), value)
        return value

    def in_yz(q):
        return chip(q // 4, q % 4, x)

    def in_row(j):
        return chip(z, y, j // 2, j % 2)

    yz = z * 4 + y

    def reduce_start(n, value):
        stat[n, 0] = value
        arb[n, yz] = value
        for d in range(1, 16):
            remote(stat.at[n, 0], arb.at[n, yz], ar_s.at[n, 0], ar_r.at[n, 0], in_yz((yz + d) % 16)).start()

    def reduce_middle(n):
        take(arb.at[n, pl.ds(0, 15)], ar_r.at[n, 0])
        value = arb[n].sum(axis=0)
        stat[n, 1] = value
        ara[n, xc] = value
        for d in range(1, 8):
            remote(stat.at[n, 1], ara.at[n, xc], ar_s.at[n, 1], ar_r.at[n, 1], in_row((xc + d) % 8)).start()

    def reduce_end(n):
        take(ara.at[n, pl.ds(0, 7)], ar_r.at[n, 1])
        return ara[n].sum(axis=0)

    def reduce_drain(n):
        sent(arb.at[n, pl.ds(0, 15)], ar_s.at[n, 0])
        sent(ara.at[n, pl.ds(0, 7)], ar_s.at[n, 1])

    pl.semaphore_wait(barrier, len(greeted))

    halo = [
        remote(cot_hbm.at[:, 0], grad_v.at[pl.ds(0, NF), NR + 1], halo_s.at[0], halo_r.at[0], above),
        remote(cot_hbm.at[:, NR - 1], grad_v.at[pl.ds(0, NF), 0], halo_s.at[1], halo_r.at[1], below),
        remote(grad_v.at[pl.ds(NF, 2), 1], grad_v.at[pl.ds(NF, 2), NR + 1], halo_s.at[2], halo_r.at[2], above),
        remote(grad_v.at[pl.ds(NF, 2), NR], grad_v.at[pl.ds(NF, 2), 0], halo_s.at[3], halo_r.at[3], below),
    ]
    up, down = (y + 1) % 4, (y + 3) % 4

    def earlier(cz, cy):
        return (cz + 3 + cy // 2) % 4

    first_to = (chip(z, up, x), chip(earlier(z, y), down, x))
    then_to = (chip(earlier(z, down), up, x), chip(z, down, x))
    quarter = NR // 2

    def first_hop(f, i):
        part = pl.ds(i * quarter, quarter)
        return remote(cot_hbm.at[f, part], relay.at[f, part], hop_s.at[0, f, i], hop_r.at[0, f, i], first_to[f])

    def second_hop(f, i):
        part = pl.ds(i * quarter, quarter)
        to = grad_v.at[NF + f, pl.ds(1 + i * quarter, quarter)]
        return remote(relay.at[f, part], to, hop_s.at[1, f, i], hop_r.at[1, f, i], then_to[f])

    def pass_on(i):
        for f in range(2):
            first_hop(f, i).wait_recv()
            second_hop(f, i).start()

    halo[0].start()
    halo[1].start()
    reduce_start(0, stacked(one, two))
    for i in range(2):
        for f in range(2):
            first_hop(f, i).start()

    copy_cot.wait()

    def bias_local(i, carry):
        return carry + fold(grad_v[i // NR, 1 + i % NR].astype(F32))

    bias = lax.fori_loop(0, NF * NR, bias_local, zero8, unroll=2)

    def clear_rows(frames):
        @pl.when(slab == 0)
        def _():
            for f in frames:
                grad_v[f, 0] = jnp.zeros((W, C), BF16)

        @pl.when(slab == 15)
        def _():
            for f in frames:
                grad_v[f, NR + 1] = jnp.zeros((W, C), BF16)

    def shifted_sum(o):
        o = o.reshape(-1, W, 3 * C)
        pixel = lax.broadcasted_iota(jnp.int32, (1, W, C), 1)
        left = pltpu.roll(o[:, :, :C], W - 1, 1)
        right = pltpu.roll(o[:, :, 2 * C :], 1, 1)
        return o[:, :, C : 2 * C] + jnp.where(pixel < W - 1, left, 0.0) + jnp.where(pixel > 0, right, 0.0)

    def act_grad(t, taps, add):
        rhs = jnp.concatenate([w_v[a * 3 + b] for a in taps for b in range(3)], axis=1)
        half = NR // 2

        def part(i, _):
            r = i * half
            lhs = jnp.concatenate(
                [
                    grad_v[t + 2 - a, pl.ds(r + 2 - b, half)].reshape(half * W, C)
                    for a in taps
                    for b in range(3)
                ],
                axis=1,
            )
            o = shifted_sum(lax.dot_general(lhs, rhs, NT_DIMS, preferred_element_type=F32))
            if add:
                o = o + ag_v[t, pl.ds(r, half)]
            ag_v[t, pl.ds(r, half)] = o
            return 0

        lax.fori_loop(0, 2, part, 0)

    copy_w.wait()
    halo[0].wait_recv()
    halo[1].wait_recv()
    clear_rows(range(NF))
    act_grad(0, (2, 1, 0), False)
    pass_on(0)
    reduce_middle(0)
    act_grad(1, (2, 1, 0), False)
    pass_on(1)

    sums = group_sum(reduce_end(0))
    mean = sums[0:1] / MEMBERS
    variance = sums[1:2] / MEMBERS - mean * mean
    inv = lax.rsqrt(variance + 1e-06)
    gain, shift = gain_ref[...], shift_ref[...]

    def activate(i, _):
        t, r = i // NR, i % NR
        normed = (act_v[t, r].astype(F32) - mean) * inv
        scaled = normed * gain + shift
        sigma = jax.nn.sigmoid(scaled)
        dv_v[t, r] = sigma * (1.0 + scaled * (1.0 - sigma))
        turned = (scaled * sigma).T
        pixel = lax.broadcasted_iota(jnp.int32, (C, W), 1)
        at_v[t, r, 0:C] = jnp.where(pixel > 0, pltpu.roll(turned, 1, 1), 0.0).astype(BF16)
        at_v[t, r, C : 2 * C] = turned.astype(BF16)
        at_v[t, r, 2 * C : 3 * C] = jnp.where(pixel < W - 1, pltpu.roll(turned, W - 1, 1), 0.0).astype(BF16)
        return 0

    lax.fori_loop(0, NF * NR, activate, 0, unroll=2)

    def weight_part(taps, frames, fresh):
        def step(t, add):
            lhs = jnp.concatenate([at_v[t, r] for r in range(NR)], axis=1)
            rhs = jnp.concatenate(
                [grad_v[t + 2 - a, 2 - b : 2 - b + NR].reshape(ROWS, C) for a in taps for b in range(3)], axis=1
            )
            o = jnp.dot(lhs, rhs, preferred_element_type=F32)
            n = 0
            for a in taps:
                for b in range(3):
                    v = o[:, n * C : (n + 1) * C].reshape(3, C, C)
                    at = pl.ds((2 - a) * 3, 3)
                    wacc[b, at] = v + wacc[b, at] if add else v
                    n += 1

        def again(t, _):
            step(t, True)
            return 0

        first, last = frames
        if fresh:
            step(first, False)
            first += 1
        lax.fori_loop(first, last, again, 0)

    half0 = core * 64
    twin = chip(z, y, x, 1 - core)
    place = (x, y, z)
    plane = (z * 4 + y, z * 4 + x, y * 4 + x)
    phases = (pl.ds(0, 3), pl.ds(3, 6))

    def on_axis(b, k):
        return (chip(z, y, k), chip(z, k, x), chip(k, y, x))[b]

    def on_plane(b, q):
        u, v = q // 4, q % 4
        return (chip(u, v, x), chip(u, y, v), chip(z, u, v))[b]

    def span_of(start, size):
        return pl.ds(pl.multiple_of(start, 16), size)

    def core_send(n):
        src = wacc.at[:, phases[n], span_of(64 - half0, 64)]
        remote(src, rs_core.at[:, phases[n]], c_s.at[n], c_r.at[n], twin).start()

    def axis_send(n):
        take(rs_core.at[:, phases[n]], c_r.at[n])
        here = span_of(half0, 64)
        for b in range(3):
            wacc[b, phases[n], here] = wacc[b, phases[n], here] + rs_core[b, phases[n]]
            for d in range(1, 4):
                k = (place[b] + d) % 4
                src = wacc.at[b, phases[n], span_of(half0 + k * 16, 16)]
                to = rs_axis.at[b, place[b], phases[n]]
                remote(src, to, x_s.at[n, b], x_r.at[n, b], on_axis(b, k)).start()

    def plane_send(b):
        for n in range(2):
            take(rs_axis.at[b, pl.ds(0, 3), phases[n]], x_r.at[n, b])
        rs_axis[b, place[b]] = wacc[b, :, span_of(half0 + place[b] * 16, 16)]
        rs_own[b] = rs_axis[b].sum(axis=0)
        for d in range(1, 16):
            p = (plane[b] + d) % 16

            @pl.when(p < 9)
            def _(p=p):
                remote(rs_own.at[b, p], rs_plane.at[b, plane[b]], p_s.at[b], p_r.at[b], on_plane(b, p)).start()

    def tile(b, p):
        return wout.at[b, p, span_of(half0 + place[b] * 16, 16)]

    def owner_sum(b):
        @pl.when(plane[b] < 9)
        def _():
            take(rs_plane.at[b, pl.ds(0, 15)], p_r.at[b])
            rs_plane[b, plane[b]] = rs_own[b, plane[b]]
            total = rs_plane[b].sum(axis=0) * SCALE
            wout[b, plane[b], span_of(half0 + place[b] * 16, 16)] = total.astype(BF16)
            for d in range(1, 16):
                p = (plane[b] + d) % 16
                remote(tile(b, plane[b]), tile(b, plane[b]), gp_s.at[b], gp_r.at[b], on_plane(b, p)).start()

    def gather_axis(b):
        tiles = wout.at[b, :, span_of(half0 + place[b] * 16, 16)]

        @pl.when(plane[b] < 9)
        def _():
            take(wout.at[b, pl.ds(0, 8), pl.ds(0, 16)], gp_r.at[b])

        @pl.when(plane[b] >= 9)
        def _():
            take(wout.at[b, :, pl.ds(0, 16)], gp_r.at[b])

        for d in range(1, 4):
            remote(tiles, tiles, gx_s.at[b], gx_r.at[b], on_axis(b, (place[b] + d) % 4)).start()

    def gather_core(b):
        take(wout.at[b, :, pl.ds(0, 48)], gx_r.at[b])
        part = wout.at[b, :, span_of(half0, 64)]
        remote(part, part, gc_s.at[b], gc_r.at[b], twin).start()

    def drain(b):
        for n in range(2):
            sent(rs_axis.at[b, pl.ds(0, 3), phases[n]], x_s.at[n, b])

        @pl.when(plane[b] < 9)
        def _():
            sent(rs_own.at[b, pl.ds(0, 8)], p_s.at[b])
            sent(wout.at[b, pl.ds(0, 5), pl.ds(0, 48)], gp_s.at[b])

        @pl.when(plane[b] >= 9)
        def _():
            sent(rs_own.at[b], p_s.at[b])

        sent(wout.at[b, :, pl.ds(0, 48)], gx_s.at[b])
        sent(wout.at[b, :, pl.ds(0, 64)], gc_s.at[b])

    weight_part((2,), (0, NF), True)
    core_send(0)
    weight_part((1, 0), (0, 2), True)
    axis_send(0)

    for i in range(2):
        for f in range(2):
            second_hop(f, i).wait_recv()
    halo[2].start()
    halo[3].start()
    act_grad(2, (2, 1), False)
    act_grad(3, (2,), False)
    halo[2].wait_recv()
    halo[3].wait_recv()
    halo[2].wait_send()
    halo[3].wait_send()
    clear_rows((NF, NF + 1))

    @pl.when(span == 7)
    def _():
        def clear(i, _):
            grad_v[NF + i // (NR + 2), i % (NR + 2)] = jnp.zeros((W, C), BF16)
            return 0

        lax.fori_loop(0, 2 * (NR + 2), clear, 0)

    weight_part((1, 0), (2, NF), False)
    core_send(1)
    act_grad(2, (0,), True)
    axis_send(1)
    act_grad(3, (1, 0), True)

    def finish(i, carry):
        t, r = i // NR, i % NR
        normed = (act_v[t, r].astype(F32) - mean) * inv
        pre = ag_v[t, r] * dv_v[t, r]
        ag_v[t, r] = pre
        return carry[0] + fold(pre * normed), carry[1] + fold(pre)

    gain_sum, shift_sum = lax.fori_loop(0, NF * NR, finish, (zero8, zero8), unroll=2)
    reduce_start(1, stacked(gain_sum, shift_sum, bias))
    for b in range(3):
        plane_send(b)
    reduce_middle(1)
    for b in range(3):
        owner_sum(b)
    total = reduce_end(1)
    sums_ref[...] = total * SCALE
    means = group_sum(total * gain) / MEMBERS
    mean_two, mean_one = means[0:1], means[1:2]

    def result(i, _):
        t, r = i // NR, i % NR
        normed = (act_v[t, r].astype(F32) - mean) * inv
        outb[t, r] = (inv * (gain * ag_v[t, r] - mean_one - normed * mean_two)).astype(BF16)
        return 0

    lax.fori_loop(0, NF * NR, result, 0, unroll=2)
    copy_out = pltpu.make_async_copy(outb, out_hbm, out_sem.at[0])
    copy_out.start()
    for b in range(3):
        gather_axis(b)
    for b in range(3):
        gather_core(b)
    for n in range(2):
        reduce_drain(n)
        sent(rs_core.at[:, phases[n]], c_s.at[n])
        halo[n].wait_send()
        for f in range(2):
            first_hop(f, n).wait_send()
            second_hop(f, n).wait_send()
    for b in range(3):
        take(wout.at[b, :, pl.ds(0, 64)], gc_r.at[b])
    copy_weights = pltpu.make_async_copy(wout, wout_hbm, out_sem.at[1])
    copy_weights.start()
    for b in range(3):
        drain(b)
    copy_out.wait()
    copy_weights.wait()


def write_out(in_hbm, w_hbm, sums_ref, out_hbm, wout_hbm, gain_ref, shift_ref, bias_ref, in_v, w_v, wide, sem):
    copy_w = pltpu.make_async_copy(w_hbm, w_v, sem.at[0])
    copy_in = pltpu.make_async_copy(in_hbm, in_v, sem.at[1])
    copy_w.start()
    copy_in.start()
    gain_ref[...] = sums_ref[0:1]
    shift_ref[...] = sums_ref[1:2]
    bias_ref[...] = sums_ref[2:3]
    copy_w.wait()
    outs = []
    for a in range(3):
        for b in range(3):
            wide[a, b] = w_v[b, (2 - a) * 3 : (3 - a) * 3].astype(F32)
        outs.append(pltpu.make_async_copy(wide.at[a], wout_hbm.at[a], sem.at[2 + a]))
        outs[-1].start()
    copy_in.wait()
    outs.append(pltpu.make_async_copy(in_v, out_hbm, sem.at[5]))
    outs[-1].start()
    for copy in outs:
        copy.wait()


def body(activations, cotangent, conv_weight, norm_gain, norm_shift):
    anywhere = pl.BlockSpec(memory_space=pl.ANY)
    vmem = pl.BlockSpec(memory_space=pltpu.VMEM)
    dma = pltpu.SemaphoreType.DMA
    input_grad, weights, sums = pl.pallas_call(
        kernel,
        out_shape=(
            jax.ShapeDtypeStruct((NF, NR, W, C), BF16),
            jax.ShapeDtypeStruct((3, 9, C, C), BF16),
            jax.ShapeDtypeStruct((8, C), F32),
        ),
        in_specs=[anywhere, anywhere, anywhere, vmem, vmem],
        out_specs=(anywhere, anywhere, vmem),
        scratch_shapes=[
            pltpu.VMEM((NF, NR, W, C), BF16),
            pltpu.VMEM((NF + 2, NR + 2, W, C), BF16),
            pltpu.VMEM((9, 3 * C, C), BF16),
            pltpu.VMEM((NF, NR, 3 * C, W), BF16),
            pltpu.VMEM((NF, NR, W, C), F32),
            pltpu.VMEM((NF, NR, W, C), F32),
            pltpu.VMEM((3, 9, C, C), F32),
            pltpu.VMEM((3, 9, 64, C), F32),
            pltpu.VMEM((3, 4, 9, 16, C), F32),
            pltpu.VMEM((3, 9, 16, C), F32),
            pltpu.VMEM((3, 16, 16, C), F32),
            pltpu.VMEM((3, 9, C, C), BF16),
            pltpu.VMEM((NF, NR, W, C), BF16),
            pltpu.VMEM((2, 2, 8, C), F32),
            pltpu.VMEM((2, 16, 8, C), F32),
            pltpu.VMEM((2, 8, 8, C), F32),
            pltpu.VMEM((2, NR, W, C), BF16),
            dma((6,)), dma((2,)), dma((4,)), dma((4,)), dma((2, 2, 2)), dma((2, 2, 2)), dma((2, 2)), dma((2, 2)),
            dma((2,)), dma((2,)), dma((2, 3)), dma((2, 3)), dma((3,)), dma((3,)),
            dma((3,)), dma((3,)), dma((3,)), dma((3,)), dma((3,)), dma((3,)),
        ],
        compiler_params=pltpu.CompilerParams(
            collective_id=0, has_side_effects=True, vmem_limit_bytes=56 * 1024 * 1024
        ),
    )(
        activations,
        cotangent,
        conv_weight.reshape(9, 3 * C, C),
        norm_gain.reshape(1, C),
        norm_shift.reshape(1, C),
    )
    per_channel = jax.ShapeDtypeStruct((1, C), F32)
    input_grad, weight_grad, gain_grad, shift_grad, bias_grad = pl.pallas_call(
        write_out,
        out_shape=(
            jax.ShapeDtypeStruct((NF, NR, W, C), BF16),
            jax.ShapeDtypeStruct((3, 3, 3, C, C), F32),
            per_channel,
            per_channel,
            per_channel,
        ),
        in_specs=[anywhere, anywhere, vmem],
        out_specs=(anywhere, anywhere, vmem, vmem, vmem),
        scratch_shapes=[
            pltpu.VMEM((NF, NR, W, C), BF16),
            pltpu.VMEM((3, 9, C, C), BF16),
            pltpu.VMEM((3, 3, 3, C, C), F32),
            dma((6,)),
        ],
        compiler_params=pltpu.CompilerParams(vmem_limit_bytes=62 * 1024 * 1024),
    )(input_grad, weights, sums)
    return input_grad, weight_grad, gain_grad.reshape(C), shift_grad.reshape(C), bias_grad.reshape(C)


def solution(mesh):
    placed = (P("span", "slab", None, None), P("span", "slab", None, None), P(), P(), P())
    return jax.shard_map(
        body,
        mesh=mesh,
        in_specs=placed,
        out_specs=(P("span", "slab", None, None), P(), P(), P(), P()),
        check_vma=False,
    )
```

```python
import jax
import jax.numpy as jnp
from jax import lax
from jax.experimental import pallas as pl
from jax.experimental.pallas import tpu as pltpu
from jax.sharding import PartitionSpec as P

MESH = pl.DeviceIdType.MESH
F32 = jnp.float32
BF16 = jnp.bfloat16
NF, NR, W, C = 4, 8, 128, 128
ROWS = NR * W
CELLS = 32 * 128 * 128
MEMBERS = CELLS * 4
SCALE = float(CELLS) ** -0.5
NT_DIMS = (((1,), (1,)), ((), ()))


def group_sum(v):
    lane = lax.broadcasted_iota(jnp.int32, v.shape, 1)
    v = v + jnp.where(lane % 2 == 0, pltpu.roll(v, C - 1, 1), pltpu.roll(v, 1, 1))
    return v + jnp.where(lane % 4 < 2, pltpu.roll(v, C - 2, 1), pltpu.roll(v, 2, 1))


def fold(v):
    return v.reshape(-1, 8, C).sum(axis=0)


def kernel(
    act_hbm, cot_hbm, w_hbm, gain_ref, shift_ref,
    outb, wout, sums_ref,
    act_v, grad_v, w_v, at_v, ag_v, dv_v, wacc, rs_core, rs_axis, rs_own, rs_plane, stat, arb, ara, relay,
    loc_sem, halo_s, halo_r, hop_s, hop_r, ar_s, ar_r,
    c_s, c_r, x_s, x_r, p_s, p_r, gp_s, gp_r, gx_s, gx_r, gc_s, gc_r,
):
    span, slab = lax.axis_index("span"), lax.axis_index("slab")
    z, y = span // 2, (span % 2) * 2 + slab // 8
    xc = slab % 8
    x, core = xc // 2, xc % 2

    def chip(cz, cy, cx, cc=core):
        return (cz * 2 + cy // 2, (cy % 2) * 8 + cx * 2 + cc)

    copies_act = [pltpu.make_async_copy(act_hbm.at[t], act_v.at[t], loc_sem.at[t]) for t in range(NF)]
    copy_cot = pltpu.make_async_copy(cot_hbm, grad_v.at[pl.ds(0, NF), pl.ds(1, NR)], loc_sem.at[NF])
    copy_w = pltpu.make_async_copy(w_hbm, w_v, loc_sem.at[NF + 1])
    for copy in copies_act:
        copy.start()
    copy_cot.start()
    copy_w.start()

    barrier = pltpu.get_barrier_semaphore()
    above = (span, (slab + 15) % 16)
    below = (span, (slab + 1) % 16)
    greeted = [above, below]
    for dz in range(4):
        for dy in range(4):
            for dx in range(4):
                if 0 in (dz, dy, dx) and (dz, dy, dx) != (0, 0, 0):
                    greeted.append(chip((z + dz) % 4, (y + dy) % 4, (x + dx) % 4))
    for dx in range(4):
        greeted.append(chip(z, y, (x + dx) % 4, 1 - core))
    for device in greeted:
        pl.semaphore_signal(barrier, inc=1, device_id=device, device_id_type=MESH)

    def remote(src, dst, send, recv, device):
        return pltpu.make_async_remote_copy(
            src_ref=src, dst_ref=dst, send_sem=send, recv_sem=recv, device_id=device, device_id_type=MESH
        )

    def take(ref, recv):
        remote(ref, ref, recv, recv, below).wait_recv()

    def sent(ref, send):
        remote(ref, ref, send, send, below).wait_send()

    zero8 = jnp.zeros((8, C), F32)
    one, two = zero8, zero8
    for t in range(NF):
        copies_act[t].wait()

        def local_sums(r, carry, t=t):
            v = act_v[t, r].astype(F32)
            return carry[0] + fold(v), carry[1] + fold(v * v)

        one, two = lax.fori_loop(0, NR, local_sums, (one, two), unroll=2)
    row = lax.broadcasted_iota(jnp.int32, (8, C), 0)

    def stacked(*sums):
        value = zero8
        for n, v in enumerate(sums):
            value = jnp.where(row == n, jnp.broadcast_to(v.sum(axis=0, keepdims=True), (8, C)), value)
        return value

    def in_yz(q):
        return chip(q // 4, q % 4, x)

    def in_row(j):
        return chip(z, y, j // 2, j % 2)

    yz = z * 4 + y

    def reduce_start(n, value):
        stat[n, 0] = value
        ara[n, xc] = value
        for d in range(1, 8):
            remote(stat.at[n, 0], ara.at[n, xc], ar_s.at[n, 0], ar_r.at[n, 0], in_row((xc + d) % 8)).start()

    def reduce_middle(n):
        take(ara.at[n, pl.ds(0, 7)], ar_r.at[n, 0])
        value = ara[n].sum(axis=0)
        stat[n, 1] = value
        arb[n, yz] = value
        for d in range(1, 16):
            remote(stat.at[n, 1], arb.at[n, yz], ar_s.at[n, 1], ar_r.at[n, 1], in_yz((yz + d) % 16)).start()

    def reduce_end(n):
        take(arb.at[n, pl.ds(0, 15)], ar_r.at[n, 1])
        return arb[n].sum(axis=0)

    def reduce_drain(n):
        sent(ara.at[n, pl.ds(0, 7)], ar_s.at[n, 0])
        sent(arb.at[n, pl.ds(0, 15)], ar_s.at[n, 1])

    pl.semaphore_wait(barrier, len(greeted))

    halo = [
        remote(cot_hbm.at[:, 0], grad_v.at[pl.ds(0, NF), NR + 1], halo_s.at[0], halo_r.at[0], above),
        remote(cot_hbm.at[:, NR - 1], grad_v.at[pl.ds(0, NF), 0], halo_s.at[1], halo_r.at[1], below),
        remote(grad_v.at[pl.ds(NF, 2), 1], grad_v.at[pl.ds(NF, 2), NR + 1], halo_s.at[2], halo_r.at[2], above),
        remote(grad_v.at[pl.ds(NF, 2), NR], grad_v.at[pl.ds(NF, 2), 0], halo_s.at[3], halo_r.at[3], below),
    ]
    up, down = (y + 1) % 4, (y + 3) % 4

    def earlier(cz, cy):
        return (cz + 3 + cy // 2) % 4

    first_to = (chip(z, up, x), chip(earlier(z, y), down, x))
    then_to = (chip(earlier(z, down), up, x), chip(z, down, x))
    half = NR // 2
    pieces = ((0, 0, half), (1, 0, 1), (1, 1, half - 1)), ((0, half, half), (1, NR - 1, 1), (1, half, half - 1))

    def first_hop(d, i):
        f, start, size = pieces[d][i]
        to = relay.at[d, f, pl.ds(start - d * half, size)]
        return remote(cot_hbm.at[f, pl.ds(start, size)], to, hop_s.at[0, d, i], hop_r.at[0, d, i], first_to[d])

    def second_hop(d, i):
        f, start, size = pieces[d][i]
        src = relay.at[d, f, pl.ds(start - d * half, size)]
        to = grad_v.at[NF + f, pl.ds(1 + start, size)]
        return remote(src, to, hop_s.at[1, d, i], hop_r.at[1, d, i], then_to[d])

    def send_first(i):
        for d in range(2):
            first_hop(d, i).start()

    def pass_on(i):
        for d in range(2):
            first_hop(d, i).wait_recv()
            second_hop(d, i).start()

    def arrive(i):
        for d in range(2):
            second_hop(d, i).wait_recv()

    reduce_start(0, stacked(one, two))
    halo[0].start()
    halo[1].start()
    send_first(0)
    send_first(1)

    copy_cot.wait()

    def bias_local(i, carry):
        return carry + fold(grad_v[i // NR, 1 + i % NR].astype(F32))

    bias = lax.fori_loop(0, NF * NR, bias_local, zero8, unroll=2)

    def clear_rows(frames):
        @pl.when(slab == 0)
        def _():
            for f in frames:
                grad_v[f, 0] = jnp.zeros((W, C), BF16)

        @pl.when(slab == 15)
        def _():
            for f in frames:
                grad_v[f, NR + 1] = jnp.zeros((W, C), BF16)

    def shifted_sum(o):
        o = o.reshape(-1, W, 3 * C)
        pixel = lax.broadcasted_iota(jnp.int32, (1, W, C), 1)
        left = pltpu.roll(o[:, :, :C], W - 1, 1)
        right = pltpu.roll(o[:, :, 2 * C :], 1, 1)
        return o[:, :, C : 2 * C] + jnp.where(pixel < W - 1, left, 0.0) + jnp.where(pixel > 0, right, 0.0)

    def act_grad(t, taps, add, halves=(0, 2)):
        rhs = jnp.concatenate([w_v[a * 3 + b] for a in taps for b in range(3)], axis=1)
        def part(i, _):
            r = i * half
            lhs = jnp.concatenate(
                [
                    grad_v[t + 2 - a, pl.ds(r + 2 - b, half)].reshape(half * W, C)
                    for a in taps
                    for b in range(3)
                ],
                axis=1,
            )
            o = shifted_sum(lax.dot_general(lhs, rhs, NT_DIMS, preferred_element_type=F32))
            if add:
                o = o + ag_v[t, pl.ds(r, half)]
            ag_v[t, pl.ds(r, half)] = o
            return 0

        lax.fori_loop(*halves, part, 0)

    reduce_middle(0)
    send_first(2)
    copy_w.wait()
    halo[0].wait_recv()
    halo[1].wait_recv()
    clear_rows(range(NF))
    act_grad(0, (2, 1, 0), False)
    pass_on(0)
    pass_on(1)
    act_grad(1, (2, 1, 0), False)
    pass_on(2)

    sums = group_sum(reduce_end(0))
    mean = sums[0:1] / MEMBERS
    variance = sums[1:2] / MEMBERS - mean * mean
    inv = lax.rsqrt(variance + 1e-06)
    gain, shift = gain_ref[...], shift_ref[...]

    def activate(i, _):
        t, r = i // NR, i % NR
        normed = (act_v[t, r].astype(F32) - mean) * inv
        scaled = normed * gain + shift
        sigma = jax.nn.sigmoid(scaled)
        dv_v[t, r] = sigma * (1.0 + scaled * (1.0 - sigma))
        turned = (scaled * sigma).T
        pixel = lax.broadcasted_iota(jnp.int32, (C, W), 1)
        at_v[t, r, 0:C] = jnp.where(pixel > 0, pltpu.roll(turned, 1, 1), 0.0).astype(BF16)
        at_v[t, r, C : 2 * C] = turned.astype(BF16)
        at_v[t, r, 2 * C : 3 * C] = jnp.where(pixel < W - 1, pltpu.roll(turned, W - 1, 1), 0.0).astype(BF16)
        return 0

    lax.fori_loop(0, NF * NR, activate, 0, unroll=4)

    def weight_part(taps, frames, fresh):
        def step(t, add):
            lhs = jnp.concatenate([at_v[t, r] for r in range(NR)], axis=1)
            rhs = jnp.concatenate(
                [grad_v[t + 2 - a, 2 - b : 2 - b + NR].reshape(ROWS, C) for a in taps for b in range(3)], axis=1
            )
            o = jnp.dot(lhs, rhs, preferred_element_type=F32)
            n = 0
            for a in taps:
                for b in range(3):
                    v = o[:, n * C : (n + 1) * C].reshape(3, C, C)
                    at = pl.ds((2 - a) * 3, 3)
                    wacc[b, at] = v + wacc[b, at] if add else v
                    n += 1

        def again(t, _):
            step(t, True)
            return 0

        first, last = frames
        if fresh:
            step(first, False)
            first += 1
        lax.fori_loop(first, last, again, 0)

    half0 = core * 64
    twin = chip(z, y, x, 1 - core)
    place = (x, y, z)
    plane = (z * 4 + y, z * 4 + x, y * 4 + x)
    phases = (pl.ds(0, 3), pl.ds(3, 6))

    def on_axis(b, k):
        return (chip(z, y, k), chip(z, k, x), chip(k, y, x))[b]

    def on_plane(b, q):
        u, v = q // 4, q % 4
        return (chip(u, v, x), chip(u, y, v), chip(z, u, v))[b]

    def span_of(start, size):
        return pl.ds(pl.multiple_of(start, 16), size)

    def core_send(n):
        src = wacc.at[:, phases[n], span_of(64 - half0, 64)]
        remote(src, rs_core.at[:, phases[n]], c_s.at[n], c_r.at[n], twin).start()

    def axis_send(n):
        take(rs_core.at[:, phases[n]], c_r.at[n])
        here = span_of(half0, 64)
        for b in range(3):
            wacc[b, phases[n], here] = wacc[b, phases[n], here] + rs_core[b, phases[n]]
            for d in range(1, 4):
                k = (place[b] + d) % 4
                src = wacc.at[b, phases[n], span_of(half0 + k * 16, 16)]
                to = rs_axis.at[b, place[b], phases[n]]
                remote(src, to, x_s.at[n, b], x_r.at[n, b], on_axis(b, k)).start()

    def plane_send(b):
        for n in range(2):
            take(rs_axis.at[b, pl.ds(0, 3), phases[n]], x_r.at[n, b])
        rs_axis[b, place[b]] = wacc[b, :, span_of(half0 + place[b] * 16, 16)]
        rs_own[b] = rs_axis[b].sum(axis=0)
        for d in range(1, 16):
            p = (plane[b] + d) % 16

            @pl.when(p < 9)
            def _(p=p):
                remote(rs_own.at[b, p], rs_plane.at[b, plane[b]], p_s.at[b], p_r.at[b], on_plane(b, p)).start()

    def tile(b, p):
        return wout.at[b, p, span_of(half0 + place[b] * 16, 16)]

    def owner_sum(b):
        @pl.when(plane[b] < 9)
        def _():
            take(rs_plane.at[b, pl.ds(0, 15)], p_r.at[b])
            rs_plane[b, plane[b]] = rs_own[b, plane[b]]
            total = rs_plane[b].sum(axis=0) * SCALE
            wout[b, plane[b], span_of(half0 + place[b] * 16, 16)] = total.astype(BF16)
            for d in range(1, 16):
                p = (plane[b] + d) % 16
                remote(tile(b, plane[b]), tile(b, plane[b]), gp_s.at[b], gp_r.at[b], on_plane(b, p)).start()

    def gather_axis(b):
        tiles = wout.at[b, :, span_of(half0 + place[b] * 16, 16)]

        @pl.when(plane[b] < 9)
        def _():
            take(wout.at[b, pl.ds(0, 8), pl.ds(0, 16)], gp_r.at[b])

        @pl.when(plane[b] >= 9)
        def _():
            take(wout.at[b, :, pl.ds(0, 16)], gp_r.at[b])

        for d in range(1, 4):
            remote(tiles, tiles, gx_s.at[b], gx_r.at[b], on_axis(b, (place[b] + d) % 4)).start()

    def gather_core(b):
        take(wout.at[b, :, pl.ds(0, 48)], gx_r.at[b])
        part = wout.at[b, :, span_of(half0, 64)]
        remote(part, part, gc_s.at[b], gc_r.at[b], twin).start()

    def drain(b):
        for n in range(2):
            sent(rs_axis.at[b, pl.ds(0, 3), phases[n]], x_s.at[n, b])

        @pl.when(plane[b] < 9)
        def _():
            sent(rs_own.at[b, pl.ds(0, 8)], p_s.at[b])
            sent(wout.at[b, pl.ds(0, 5), pl.ds(0, 48)], gp_s.at[b])

        @pl.when(plane[b] >= 9)
        def _():
            sent(rs_own.at[b], p_s.at[b])

        sent(wout.at[b, :, pl.ds(0, 48)], gx_s.at[b])
        sent(wout.at[b, :, pl.ds(0, 64)], gc_s.at[b])

    weight_part((2,), (0, NF), True)
    core_send(0)
    arrive(0)
    arrive(1)
    halo[2].start()
    halo[3].start()
    weight_part((1, 0), (0, 2), True)
    axis_send(0)
    halo[2].wait_recv()
    halo[3].wait_recv()
    halo[2].wait_send()
    halo[3].wait_send()
    clear_rows((NF, NF + 1))

    def clear_frame(f):
        @pl.when(span == 7)
        def _():
            def clear(i, _):
                grad_v[f, i] = jnp.zeros((W, C), BF16)
                return 0

            lax.fori_loop(0, NR + 2, clear, 0)

    clear_frame(NF)
    weight_part((1, 0), (2, 3), False)
    arrive(2)
    clear_frame(NF + 1)
    weight_part((1, 0), (3, NF), False)
    core_send(1)
    act_grad(3, (2, 1, 0), False)
    axis_send(1)
    act_grad(2, (2, 1, 0), False)

    def finish(i, carry):
        t, r = i // NR, i % NR
        normed = (act_v[t, r].astype(F32) - mean) * inv
        pre = ag_v[t, r] * dv_v[t, r]
        ag_v[t, r] = pre
        return carry[0] + fold(pre * normed), carry[1] + fold(pre)

    gain_sum, shift_sum = lax.fori_loop(0, NF * NR, finish, (zero8, zero8), unroll=2)
    reduce_start(1, stacked(gain_sum, shift_sum, bias))
    for b in range(3):
        plane_send(b)
    reduce_middle(1)
    for b in range(3):
        owner_sum(b)
    total = reduce_end(1)
    sums_ref[...] = total * SCALE
    means = group_sum(total * gain) / MEMBERS
    mean_two, mean_one = means[0:1], means[1:2]

    def result(i, _):
        t, r = i // NR, i % NR
        normed = (act_v[t, r].astype(F32) - mean) * inv
        outb[t, r] = (inv * (gain * ag_v[t, r] - mean_one - normed * mean_two)).astype(BF16)
        return 0

    lax.fori_loop(0, NF * NR, result, 0, unroll=2)
    for b in range(3):
        gather_axis(b)
    for b in range(3):
        gather_core(b)
    for n in range(2):
        reduce_drain(n)
        sent(rs_core.at[:, phases[n]], c_s.at[n])
        halo[n].wait_send()
        for i in range(3):
            first_hop(n, i).wait_send()
            second_hop(n, i).wait_send()
    for b in range(3):
        take(wout.at[b, :, pl.ds(0, 64)], gc_r.at[b])
    for b in range(3):
        drain(b)


def write_out(in_ref, w_ref, sums_ref, out_hbm, wout_hbm, gain_ref, shift_ref, bias_ref, wide, sem):
    outs = []
    for a in range(3):
        for b in range(3):
            wide[a, b] = w_ref[b, (2 - a) * 3 : (3 - a) * 3].astype(F32)
        outs.append(pltpu.make_async_copy(wide.at[a], wout_hbm.at[a], sem.at[a]))
        outs[-1].start()
    outs.append(pltpu.make_async_copy(in_ref, out_hbm, sem.at[3]))
    outs[-1].start()
    gain_ref[...] = sums_ref[0:1]
    shift_ref[...] = sums_ref[1:2]
    bias_ref[...] = sums_ref[2:3]
    for copy in outs:
        copy.wait()


def body(activations, cotangent, conv_weight, norm_gain, norm_shift):
    anywhere = pl.BlockSpec(memory_space=pl.ANY)
    vmem = pl.BlockSpec(memory_space=pltpu.VMEM)
    dma = pltpu.SemaphoreType.DMA
    input_grad, weights, sums = pl.pallas_call(
        kernel,
        out_shape=(
            pltpu.VMEM((NF, NR, W, C), BF16),
            pltpu.VMEM((3, 9, C, C), BF16),
            pltpu.VMEM((8, C), F32),
        ),
        in_specs=[anywhere, anywhere, anywhere, vmem, vmem],
        out_specs=(vmem, vmem, vmem),
        scratch_shapes=[
            pltpu.VMEM((NF, NR, W, C), BF16),
            pltpu.VMEM((NF + 2, NR + 2, W, C), BF16),
            pltpu.VMEM((9, 3 * C, C), BF16),
            pltpu.VMEM((NF, NR, 3 * C, W), BF16),
            pltpu.VMEM((NF, NR, W, C), F32),
            pltpu.VMEM((NF, NR, W, C), F32),
            pltpu.VMEM((3, 9, C, C), F32),
            pltpu.VMEM((3, 9, 64, C), F32),
            pltpu.VMEM((3, 4, 9, 16, C), F32),
            pltpu.VMEM((3, 9, 16, C), F32),
            pltpu.VMEM((3, 16, 16, C), F32),
            pltpu.VMEM((2, 2, 8, C), F32),
            pltpu.VMEM((2, 16, 8, C), F32),
            pltpu.VMEM((2, 8, 8, C), F32),
            pltpu.VMEM((2, 2, NR // 2, W, C), BF16),
            dma((6,)), dma((4,)), dma((4,)), dma((2, 2, 3)), dma((2, 2, 3)), dma((2, 2)), dma((2, 2)),
            dma((2,)), dma((2,)), dma((2, 3)), dma((2, 3)), dma((3,)), dma((3,)),
            dma((3,)), dma((3,)), dma((3,)), dma((3,)), dma((3,)), dma((3,)),
        ],
        compiler_params=pltpu.CompilerParams(
            collective_id=0, has_side_effects=True, vmem_limit_bytes=65_000_000
        ),
    )(
        activations,
        cotangent,
        conv_weight.reshape(9, 3 * C, C),
        norm_gain.reshape(1, C),
        norm_shift.reshape(1, C),
    )
    per_channel = jax.ShapeDtypeStruct((1, C), F32)
    input_grad, weight_grad, gain_grad, shift_grad, bias_grad = pl.pallas_call(
        write_out,
        out_shape=(
            jax.ShapeDtypeStruct((NF, NR, W, C), BF16),
            jax.ShapeDtypeStruct((3, 3, 3, C, C), F32),
            per_channel,
            per_channel,
            per_channel,
        ),
        in_specs=[vmem, vmem, vmem],
        out_specs=(anywhere, anywhere, vmem, vmem, vmem),
        scratch_shapes=[pltpu.VMEM((3, 3, 3, C, C), F32), dma((4,))],
        compiler_params=pltpu.CompilerParams(vmem_limit_bytes=16 * 1024 * 1024),
    )(input_grad, weights, sums)
    return input_grad, weight_grad, gain_grad.reshape(C), shift_grad.reshape(C), bias_grad.reshape(C)


def solution(mesh):
    placed = (P("span", "slab", None, None), P("span", "slab", None, None), P(), P(), P())
    return jax.shard_map(
        body,
        mesh=mesh,
        in_specs=placed,
        out_specs=(P("span", "slab", None, None), P(), P(), P(), P()),
        check_vma=False,
    )
```

```python
import jax
import jax.numpy as jnp
from jax import lax
from jax.experimental import pallas as pl
from jax.experimental.pallas import tpu as pltpu
from jax.sharding import PartitionSpec as P

MESH = pl.DeviceIdType.MESH
F32 = jnp.float32
BF16 = jnp.bfloat16
NF, NR, W, C = 4, 8, 128, 128
ROWS = NR * W
CELLS = 32 * 128 * 128
MEMBERS = CELLS * 4
SCALE = float(CELLS) ** -0.5
SENT = 2 * NF * 64 + 2 * 2 * NR * 64 + 2 * (7 + 15) * 4 + 27 * 64 + 3 * 27 * 48 + 27 * 24 + 27 * 32
GROUPS = 3
NT_DIMS = (((1,), (1,)), ((), ()))


def group_sum(v):
    lane = lax.broadcasted_iota(jnp.int32, v.shape, 1)
    v = v + jnp.where(lane % 2 == 0, pltpu.roll(v, C - 1, 1), pltpu.roll(v, 1, 1))
    return v + jnp.where(lane % 4 < 2, pltpu.roll(v, C - 2, 1), pltpu.roll(v, 2, 1))


def fold(v):
    return v.reshape(-1, 8, C).sum(axis=0)


def kernel(
    act_hbm, cot_hbm, w_hbm, gain_ref, shift_ref,
    outb, wout, sums_ref,
    act_v, grad_v, w_v, at_v, ag_v, dv_v, wacc, rs_core, rs_axis, stat, arb, ara, relay,
    all_sent, loc_sem, send_sem, halo_r, hop_r, ar_r, c_r, x_r, y_r, z_r, gx_r, gc_r,
):
    span, slab = lax.axis_index("span"), lax.axis_index("slab")
    z, y = span // 2, (span % 2) * 2 + slab // 8
    xc = slab % 8
    x, core = xc // 2, xc % 2

    def chip(cz, cy, cx, cc=core):
        return (cz * 2 + cy // 2, (cy % 2) * 8 + cx * 2 + cc)

    copies_act = [pltpu.make_async_copy(act_hbm.at[t], act_v.at[t], loc_sem.at[t]) for t in range(NF)]
    copy_cot = pltpu.make_async_copy(cot_hbm, grad_v.at[pl.ds(0, NF), pl.ds(1, NR)], loc_sem.at[NF])
    copy_w = pltpu.make_async_copy(w_hbm, w_v, loc_sem.at[NF + 1])
    for copy in copies_act:
        copy.start()
    copy_cot.start()
    copy_w.start()

    barrier = pltpu.get_barrier_semaphore()
    above = (span, (slab + 15) % 16)
    below = (span, (slab + 1) % 16)
    greeted = [above, below]
    greeted += [chip((z + d // 4) % 4, (y + d % 4) % 4, x) for d in range(1, 16)]
    greeted += [chip(z, y, (x + d // 2) % 4, (core + d) % 2) for d in range(1, 8)]
    for device in greeted:
        pl.semaphore_signal(barrier, inc=1, device_id=device, device_id_type=MESH)

    def remote(src, dst, send, recv, device):
        return pltpu.make_async_remote_copy(
            src_ref=src, dst_ref=dst, send_sem=send, recv_sem=recv, device_id=device, device_id_type=MESH
        )

    def take(ref, recv):
        remote(ref, ref, recv, recv, below).wait_recv()

    def sent(ref, send):
        remote(ref, ref, send, send, below).wait_send()

    zero8 = jnp.zeros((8, C), F32)
    one, two = zero8, zero8
    for t in range(NF):
        copies_act[t].wait()

        def local_sums(r, carry, t=t):
            v = act_v[t, r].astype(F32)
            return carry[0] + fold(v), carry[1] + fold(v * v)

        one, two = lax.fori_loop(0, NR, local_sums, (one, two), unroll=2)
    row = lax.broadcasted_iota(jnp.int32, (4, C), 0)

    def stacked(*sums):
        value = jnp.zeros((4, C), F32)
        for n, v in enumerate(sums):
            value = jnp.where(row == n, jnp.broadcast_to(v.sum(axis=0, keepdims=True), (4, C)), value)
        return value

    def in_yz(q):
        return chip(q // 4, q % 4, x)

    def in_row(j):
        return chip(z, y, j // 2, j % 2)

    yz = z * 4 + y

    def reduce_start(n, value):
        stat[n, 0] = value
        ara[n, xc] = value
        for d in range(1, 8):
            remote(stat.at[n, 0], ara.at[n, xc], send_sem.at[0], ar_r.at[n, 0], in_row((xc + d) % 8)).start()

    def reduce_middle(n):
        take(ara.at[n, pl.ds(0, 7)], ar_r.at[n, 0])
        value = ara[n].sum(axis=0)
        stat[n, 1] = value
        arb[n, yz] = value
        for d in range(1, 16):
            remote(stat.at[n, 1], arb.at[n, yz], send_sem.at[0], ar_r.at[n, 1], in_yz((yz + d) % 16)).start()

    def reduce_end(n):
        take(arb.at[n, pl.ds(0, 15)], ar_r.at[n, 1])
        return arb[n].sum(axis=0)

    pl.semaphore_wait(barrier, len(greeted))

    halo = [
        remote(cot_hbm.at[:, 0], grad_v.at[pl.ds(0, NF), NR + 1], send_sem.at[0], halo_r.at[0], above),
        remote(cot_hbm.at[:, NR - 1], grad_v.at[pl.ds(0, NF), 0], send_sem.at[0], halo_r.at[1], below),
        remote(grad_v.at[NF, 1], grad_v.at[NF, NR + 1], send_sem.at[1], halo_r.at[2], above),
        remote(grad_v.at[NF, NR], grad_v.at[NF, 0], send_sem.at[2], halo_r.at[3], below),
        remote(grad_v.at[NF + 1, 1], grad_v.at[NF + 1, NR + 1], send_sem.at[3], halo_r.at[4], above),
        remote(grad_v.at[NF + 1, NR], grad_v.at[NF + 1, 0], send_sem.at[4], halo_r.at[5], below),
    ]
    up, down = (y + 1) % 4, (y + 3) % 4

    def earlier(cz, cy):
        return (cz + 3 + cy // 2) % 4

    first_to = (chip(z, up, x), chip(earlier(z, y), down, x))
    then_to = (chip(earlier(z, down), up, x), chip(z, down, x))
    half = NR // 2
    pieces = ((0, 0, half), (1, 0, 1), (1, 1, half - 1)), ((0, half, half), (1, NR - 1, 1), (1, half, half - 1))

    def first_hop(d, i):
        f, start, size = pieces[d][i]
        to = relay.at[d, f, pl.ds(start - d * half, size)]
        return remote(cot_hbm.at[f, pl.ds(start, size)], to, send_sem.at[0], hop_r.at[0, d, i], first_to[d])

    def second_hop(d, i):
        f, start, size = pieces[d][i]
        src = relay.at[d, f, pl.ds(start - d * half, size)]
        to = grad_v.at[NF + f, pl.ds(1 + start, size)]
        return remote(src, to, send_sem.at[0], hop_r.at[1, d, i], then_to[d])

    def send_first(i):
        for d in range(2):
            first_hop(d, i).start()

    def pass_on(i):
        for d in range(2):
            first_hop(d, i).wait_recv()
            second_hop(d, i).start()

    def arrive(i):
        for d in range(2):
            second_hop(d, i).wait_recv()

    reduce_start(0, stacked(one, two))
    halo[0].start()
    halo[1].start()
    send_first(0)
    send_first(1)

    copy_cot.wait()

    def bias_local(i, carry):
        return carry + fold(grad_v[i // NR, 1 + i % NR].astype(F32))

    bias = lax.fori_loop(0, NF * NR, bias_local, zero8, unroll=2)

    def clear_rows(frames):
        @pl.when(slab == 0)
        def _():
            for f in frames:
                grad_v[f, 0] = jnp.zeros((W, C), BF16)

        @pl.when(slab == 15)
        def _():
            for f in frames:
                grad_v[f, NR + 1] = jnp.zeros((W, C), BF16)

    def shifted_sum(o):
        o = o.reshape(-1, W, 3 * C)
        pixel = lax.broadcasted_iota(jnp.int32, (1, W, C), 1)
        left = pltpu.roll(o[:, :, :C], W - 1, 1)
        right = pltpu.roll(o[:, :, 2 * C :], 1, 1)
        return o[:, :, C : 2 * C] + jnp.where(pixel < W - 1, left, 0.0) + jnp.where(pixel > 0, right, 0.0)

    def act_grad(t, taps, add, parts=((0, 4), (4, 4))):
        rhs = jnp.concatenate([w_v[a * 3 + b] for a in taps for b in range(3)], axis=1)
        for r, n in parts:
            lhs = jnp.concatenate(
                [
                    grad_v[t + 2 - a, r + 2 - b : r + 2 - b + n].reshape(n * W, C)
                    for a in taps
                    for b in range(3)
                ],
                axis=1,
            )
            o = shifted_sum(lax.dot_general(lhs, rhs, NT_DIMS, preferred_element_type=F32))
            if add:
                o = o + ag_v[t, r : r + n]
            ag_v[t, r : r + n] = o

    inner, outer = ((2, 4),), ((0, 2), (6, 2))
    first, second = ((0, 4),), ((4, 4),)
    copy_w.wait()
    act_grad(0, (2, 1, 0), False, inner)
    act_grad(1, (2, 1, 0), False, inner)
    reduce_middle(0)
    send_first(2)
    halo[0].wait_recv()
    halo[1].wait_recv()
    clear_rows(range(NF))
    act_grad(0, (2, 1, 0), False, outer)
    pass_on(0)
    act_grad(1, (2, 1, 0), False, outer)
    pass_on(1)
    act_grad(3, (2,), False)
    sums = group_sum(reduce_end(0))
    mean = sums[0:1] / MEMBERS
    variance = sums[1:2] / MEMBERS - mean * mean
    inv = lax.rsqrt(variance + 1e-06)
    gain, shift = gain_ref[...], shift_ref[...]

    pixel = lax.broadcasted_iota(jnp.int32, (C, W), 1)

    def activate(t):
        for r in range(NR):
            normed = (act_v[t, r].astype(F32) - mean) * inv
            scaled = normed * gain + shift
            sigma = jax.nn.sigmoid(scaled)
            dv_v[t, r] = sigma * (1.0 + scaled * (1.0 - sigma))
            turned = (scaled * sigma).T
            at_v[t, r, 0:C] = jnp.where(pixel > 0, pltpu.roll(turned, 1, 1), 0.0).astype(BF16)
            at_v[t, r, C : 2 * C] = turned.astype(BF16)
            at_v[t, r, 2 * C : 3 * C] = jnp.where(pixel < W - 1, pltpu.roll(turned, W - 1, 1), 0.0).astype(BF16)

    def weight_part(taps, t, add):
        lhs = jnp.concatenate([at_v[t, r] for r in range(NR)], axis=1)
        rhs = jnp.concatenate(
            [grad_v[t + 2 - a, 2 - b : 2 - b + NR].reshape(ROWS, C) for a in taps for b in range(3)], axis=1
        )
        o = jnp.dot(lhs, rhs, preferred_element_type=F32)
        n = 0
        for a in taps:
            for b in range(3):
                v = o[:, n * C : (n + 1) * C].reshape(3, C, C)
                at = pl.ds((2 - a) * 3, 3)
                wacc[b, at] = v + wacc[b, at] if add else v
                n += 1

    half0 = core * 64
    twin = chip(z, y, x, 1 - core)
    place = (x, y, z)
    phases = (pl.ds(0, 3), pl.ds(3, 3), pl.ds(6, 3))
    groups = ((0, 3), (3, 6), (6, 9)) if GROUPS == 3 else ((0, 6), (6, 9))
    members = ((0,), (1,), (2,)) if GROUPS == 3 else ((0, 1), (2,))

    def on_axis(b, k):
        return (chip(z, y, k), chip(z, k, x), chip(k, y, x))[b]

    def span_of(start, size):
        return pl.ds(pl.multiple_of(start, 16), size)

    def core_send(n):
        src = wacc.at[:, phases[n], span_of(64 - half0, 64)]
        remote(src, rs_core.at[:, phases[n]], send_sem.at[0], c_r.at[n], twin).start()

    def axis_send(n):
        take(rs_core.at[:, phases[n]], c_r.at[n])
        here = span_of(half0, 64)
        for b in range(3):
            wacc[b, phases[n], here] = wacc[b, phases[n], here] + rs_core[b, phases[n]]
            for d in range(1, 4):
                k = (place[b] + d) % 4
                src = wacc.at[b, phases[n], span_of(half0 + k * 16, 16)]
                to = rs_axis.at[0, b, place[b], phases[n]]
                remote(src, to, send_sem.at[0], x_r.at[n, b], on_axis(b, k)).start()

    def mine(b):
        return span_of(half0 + place[b] * 16, 16)

    def exchange(k, g, b, value, recv):
        lo, hi = groups[g]
        axis = (b + k) % 3
        slot = rs_axis.at[k, b, place[axis], pl.ds(lo, hi - lo)]
        slot[...] = value
        for d in range(1, 4):
            remote(slot, slot, send_sem.at[0], recv.at[g, b], on_axis(axis, (place[axis] + d) % 4)).start()

    def along_second(g, b):
        lo, hi = groups[g]
        for n in members[g]:
            take(rs_axis.at[0, b, pl.ds(0, 3), phases[n]], x_r.at[n, b])
        rs_axis[0, b, place[b], pl.ds(lo, hi - lo)] = wacc[b, lo:hi, mine(b)]
        exchange(1, g, b, rs_axis[0, b, :, lo:hi].sum(axis=0), y_r)

    def along_third(g, b):
        lo, hi = groups[g]
        take(rs_axis.at[1, b, pl.ds(0, 3), pl.ds(lo, hi - lo)], y_r.at[g, b])
        exchange(2, g, b, rs_axis[1, b, :, lo:hi].sum(axis=0), z_r)

    def gather_axis(g, b):
        lo, hi = groups[g]
        take(rs_axis.at[2, b, pl.ds(0, 3), pl.ds(lo, hi - lo)], z_r.at[g, b])
        total = rs_axis[2, b, :, lo:hi].sum(axis=0) * SCALE
        wout[b, lo:hi, mine(b)] = total.astype(BF16)
        tiles = wout.at[b, pl.ds(lo, hi - lo), mine(b)]
        for d in range(1, 4):
            remote(tiles, tiles, send_sem.at[0], gx_r.at[g, b], on_axis(b, (place[b] + d) % 4)).start()

    def gather_core(g, b):
        lo, hi = groups[g]
        take(wout.at[b, pl.ds(lo, hi - lo), pl.ds(0, 48)], gx_r.at[g, b])
        part = wout.at[b, pl.ds(lo, hi - lo), span_of(half0, 64)]
        remote(part, part, send_sem.at[0], gc_r.at[g, b], twin).start()

    def complete(g, b):
        lo, hi = groups[g]
        take(wout.at[b, pl.ds(lo, hi - lo), pl.ds(0, 64)], gc_r.at[g, b])

    def clear_frame(f):
        @pl.when(span == 7)
        def _():
            def clear(i, _):
                grad_v[f, i] = jnp.zeros((W, C), BF16)
                return 0

            lax.fori_loop(0, NR + 2, clear, 0)

    activate(0)
    pass_on(2)
    weight_part((2,), 0, False)
    activate(1)
    weight_part((2,), 1, True)
    activate(2)
    arrive(0)
    halo[2].start()
    halo[3].start()
    weight_part((2,), 2, True)
    activate(3)
    weight_part((2,), 3, True)
    core_send(0)
    arrive(1)
    halo[4].start()
    halo[5].start()
    for t in range(3):
        weight_part((1,), t, t > 0)
    for t in range(2):
        weight_part((0,), t, t > 0)
    axis_send(0)
    for n in (2, 3):
        halo[n].wait_recv()
        halo[n].wait_send()
    clear_rows((NF,))
    clear_frame(NF)
    weight_part((1,), 3, True)
    core_send(1)
    weight_part((0,), 2, True)
    arrive(2)
    for n in (4, 5):
        halo[n].wait_recv()
        halo[n].wait_send()
    clear_rows((NF + 1,))
    clear_frame(NF + 1)
    weight_part((0,), 3, True)
    core_send(2)
    act_grad(3, (1, 0), True, first)
    axis_send(1)
    axis_send(2)
    act_grad(3, (1, 0), True, second)
    act_grad(2, (2, 1, 0), False, first)
    act_grad(2, (2, 1, 0), False, second)

    def finish(i, carry):
        t, r = i // NR, i % NR
        normed = (act_v[t, r].astype(F32) - mean) * inv
        pre = ag_v[t, r] * dv_v[t, r]
        ag_v[t, r] = pre
        return carry[0] + fold(pre * normed), carry[1] + fold(pre)

    gain_sum, shift_sum = lax.fori_loop(0, NF * NR, finish, (zero8, zero8), unroll=2)
    reduce_start(1, stacked(gain_sum, shift_sum, bias))
    for g in range(GROUPS):
        for b in range(3):
            along_second(g, b)
    reduce_middle(1)
    for g in range(GROUPS):
        for b in range(3):
            along_third(g, b)
    for g in range(GROUPS):
        for b in range(3):
            gather_axis(g, b)
    total = reduce_end(1)
    sums_ref[...] = total * SCALE
    means = group_sum(total * gain) / MEMBERS
    mean_two, mean_one = means[0:1], means[1:2]

    def result(i, _):
        t, r = i // NR, i % NR
        normed = (act_v[t, r].astype(F32) - mean) * inv
        outb[t, r] = (inv * (gain * ag_v[t, r] - mean_one - normed * mean_two)).astype(BF16)
        return 0

    lax.fori_loop(0, NF * NR, result, 0, unroll=2)
    for g in range(GROUPS):
        for b in range(3):
            gather_core(g, b)
    for g in range(GROUPS):
        for b in range(3):
            complete(g, b)
    sent(all_sent, send_sem.at[0])


def write_out(in_ref, w_ref, sums_ref, out_hbm, wout_hbm, gain_ref, shift_ref, bias_ref, wide, sem):
    outs = []
    for a in range(3):
        for b in range(3):
            wide[a, b] = w_ref[b, (2 - a) * 3 : (3 - a) * 3].astype(F32)
        outs.append(pltpu.make_async_copy(wide.at[a], wout_hbm.at[a], sem.at[a]))
        outs[-1].start()
    outs.append(pltpu.make_async_copy(in_ref, out_hbm, sem.at[3]))
    outs[-1].start()
    gain_ref[...] = sums_ref[0:1]
    shift_ref[...] = sums_ref[1:2]
    bias_ref[...] = sums_ref[2:3]
    for copy in outs:
        copy.wait()


def body(activations, cotangent, conv_weight, norm_gain, norm_shift):
    anywhere = pl.BlockSpec(memory_space=pl.ANY)
    vmem = pl.BlockSpec(memory_space=pltpu.VMEM)
    dma = pltpu.SemaphoreType.DMA
    input_grad, weights, sums = pl.pallas_call(
        kernel,
        out_shape=(
            pltpu.VMEM((NF, NR, W, C), BF16),
            pltpu.VMEM((3, 9, C, C), BF16),
            pltpu.VMEM((4, C), F32),
        ),
        in_specs=[anywhere, anywhere, anywhere, vmem, vmem],
        out_specs=(vmem, vmem, vmem),
        scratch_shapes=[
            pltpu.VMEM((NF, NR, W, C), BF16),
            pltpu.VMEM((NF + 2, NR + 2, W, C), BF16),
            pltpu.VMEM((9, 3 * C, C), BF16),
            pltpu.VMEM((NF, NR, 3 * C, W), BF16),
            pltpu.VMEM((NF, NR, W, C), F32),
            pltpu.VMEM((NF, NR, W, C), F32),
            pltpu.VMEM((3, 9, C, C), F32),
            pltpu.VMEM((3, 9, 64, C), F32),
            pltpu.VMEM((3, 3, 4, 9, 16, C), F32),
            pltpu.VMEM((2, 2, 4, C), F32),
            pltpu.VMEM((2, 16, 4, C), F32),
            pltpu.VMEM((2, 8, 4, C), F32),
            pltpu.VMEM((2, 2, NR // 2, W, C), BF16),
            pltpu.VMEM((SENT, C), F32),
            dma((6,)), dma((5,)), dma((6,)), dma((2, 2, 3)), dma((2, 2)), dma((3,)), dma((3, 3)),
            dma((GROUPS, 3)), dma((GROUPS, 3)), dma((GROUPS, 3)), dma((GROUPS, 3)),
        ],
        compiler_params=pltpu.CompilerParams(
            collective_id=0, has_side_effects=True, vmem_limit_bytes=65_000_000
        ),
    )(
        activations,
        cotangent,
        conv_weight.reshape(9, 3 * C, C),
        norm_gain.reshape(1, C),
        norm_shift.reshape(1, C),
    )
    per_channel = jax.ShapeDtypeStruct((1, C), F32)
    input_grad, weight_grad, gain_grad, shift_grad, bias_grad = pl.pallas_call(
        write_out,
        out_shape=(
            jax.ShapeDtypeStruct((NF, NR, W, C), BF16),
            jax.ShapeDtypeStruct((3, 3, 3, C, C), F32),
            per_channel,
            per_channel,
            per_channel,
        ),
        in_specs=[vmem, vmem, vmem],
        out_specs=(anywhere, anywhere, vmem, vmem, vmem),
        scratch_shapes=[pltpu.VMEM((3, 3, 3, C, C), F32), dma((4,))],
        compiler_params=pltpu.CompilerParams(vmem_limit_bytes=16 * 1024 * 1024),
    )(input_grad, weights, sums)
    return input_grad, weight_grad, gain_grad.reshape(C), shift_grad.reshape(C), bias_grad.reshape(C)


def solution(mesh):
    placed = (P("span", "slab", None, None), P("span", "slab", None, None), P(), P(), P())
    return jax.shard_map(
        body,
        mesh=mesh,
        in_specs=placed,
        out_specs=(P("span", "slab", None, None), P(), P(), P(), P()),
        check_vma=False,
    )
```

```python
import jax
import jax.numpy as jnp
from jax import lax
from jax.experimental import pallas as pl
from jax.experimental.pallas import tpu as pltpu
from jax.sharding import PartitionSpec as P

MESH = pl.DeviceIdType.MESH
F32 = jnp.float32
BF16 = jnp.bfloat16
NF, NR, W, C = 4, 8, 128, 128
ROWS = NR * W
CELLS = 32 * 128 * 128
MEMBERS = CELLS * 4
SCALE = float(CELLS) ** -0.5
SENT = 2 * NF * 64 + 2 * NR * 64 + 2 * (7 + 15) * 4 + 27 * 64 + 3 * 27 * 48 + 27 * 24 + 27 * 32
GROUPS = 3
NT_DIMS = (((1,), (1,)), ((), ()))


def group_sum(v):
    lane = lax.broadcasted_iota(jnp.int32, v.shape, 1)
    v = v + jnp.where(lane % 2 == 0, pltpu.roll(v, C - 1, 1), pltpu.roll(v, 1, 1))
    return v + jnp.where(lane % 4 < 2, pltpu.roll(v, C - 2, 1), pltpu.roll(v, 2, 1))


def fold(v):
    return v.reshape(-1, 8, C).sum(axis=0)


def kernel(
    act_hbm, cot_hbm, w_hbm, gain_ref, shift_ref,
    outb, wide, sums_ref,
    act_v, grad_v, w_v, at_v, ag_v, dv_v, wacc, rs_core, rs_axis, wout, stat, arb, ara,
    all_sent, loc_sem, send_sem, halo_r, frame_r, ar_r, c_r, x_r, y_r, z_r, gx_r, gc_r,
):
    span, slab = lax.axis_index("span"), lax.axis_index("slab")
    z, y = span // 2, (span % 2) * 2 + slab // 8
    xc = slab % 8
    x, core = xc // 2, xc % 2

    def chip(cz, cy, cx, cc=core):
        return (cz * 2 + cy // 2, (cy % 2) * 8 + cx * 2 + cc)

    copies_act = [pltpu.make_async_copy(act_hbm.at[t], act_v.at[t], loc_sem.at[t]) for t in range(NF)]
    copy_cot = pltpu.make_async_copy(cot_hbm, grad_v.at[pl.ds(0, NF), pl.ds(1, NR)], loc_sem.at[NF])
    copy_w = pltpu.make_async_copy(w_hbm, w_v, loc_sem.at[NF + 1])
    for copy in copies_act:
        copy.start()
    copy_cot.start()
    copy_w.start()

    barrier = pltpu.get_barrier_semaphore()
    above = (span, (slab + 15) % 16)
    below = (span, (slab + 1) % 16)
    greeted = [above, below]
    greeted += [chip((z + d // 4) % 4, (y + d % 4) % 4, x) for d in range(1, 16)]
    greeted += [chip(z, y, (x + d // 2) % 4, (core + d) % 2) for d in range(1, 8)]
    for device in greeted:
        pl.semaphore_signal(barrier, inc=1, device_id=device, device_id_type=MESH)

    def remote(src, dst, send, recv, device):
        return pltpu.make_async_remote_copy(
            src_ref=src, dst_ref=dst, send_sem=send, recv_sem=recv, device_id=device, device_id_type=MESH
        )

    def take(ref, recv):
        remote(ref, ref, recv, recv, below).wait_recv()

    def sent(ref, send):
        remote(ref, ref, send, send, below).wait_send()

    zero8 = jnp.zeros((8, C), F32)
    one, two = zero8, zero8
    for t in range(NF):
        copies_act[t].wait()

        def local_sums(r, carry, t=t):
            v = act_v[t, r].astype(F32)
            return carry[0] + fold(v), carry[1] + fold(v * v)

        one, two = lax.fori_loop(0, NR, local_sums, (one, two), unroll=2)
    row = lax.broadcasted_iota(jnp.int32, (4, C), 0)

    def stacked(*sums):
        value = jnp.zeros((4, C), F32)
        for n, v in enumerate(sums):
            value = jnp.where(row == n, jnp.broadcast_to(v.sum(axis=0, keepdims=True), (4, C)), value)
        return value

    def in_yz(q):
        return chip(q // 4, q % 4, x)

    def in_row(j):
        return chip(z, y, j // 2, j % 2)

    yz = z * 4 + y

    def reduce_start(n, value):
        stat[n, 0] = value
        ara[n, xc] = value
        for d in range(1, 8):
            remote(stat.at[n, 0], ara.at[n, xc], send_sem.at[0], ar_r.at[n, 0], in_row((xc + d) % 8)).start()

    def reduce_middle(n):
        take(ara.at[n, pl.ds(0, 7)], ar_r.at[n, 0])
        value = ara[n].sum(axis=0)
        stat[n, 1] = value
        arb[n, yz] = value
        for d in range(1, 16):
            remote(stat.at[n, 1], arb.at[n, yz], send_sem.at[0], ar_r.at[n, 1], in_yz((yz + d) % 16)).start()

    def reduce_end(n):
        take(arb.at[n, pl.ds(0, 15)], ar_r.at[n, 1])
        return arb[n].sum(axis=0)

    pl.semaphore_wait(barrier, len(greeted))

    halo = [
        remote(cot_hbm.at[:, 0], grad_v.at[pl.ds(0, NF), NR + 1], send_sem.at[0], halo_r.at[0], above),
        remote(cot_hbm.at[:, NR - 1], grad_v.at[pl.ds(0, NF), 0], send_sem.at[0], halo_r.at[1], below),
        remote(grad_v.at[NF, 1], grad_v.at[NF, NR + 1], send_sem.at[1], halo_r.at[2], above),
        remote(grad_v.at[NF, NR], grad_v.at[NF, 0], send_sem.at[2], halo_r.at[3], below),
        remote(grad_v.at[NF + 1, 1], grad_v.at[NF + 1, NR + 1], send_sem.at[3], halo_r.at[4], above),
        remote(grad_v.at[NF + 1, NR], grad_v.at[NF + 1, 0], send_sem.at[4], halo_r.at[5], below),
    ]
    before = ((span + 7) % 8, slab)
    half = NR // 2

    def frame_send(f, start, size, n):
        to = grad_v.at[NF + f, pl.ds(1 + start, size)]
        remote(cot_hbm.at[f, pl.ds(start, size)], to, send_sem.at[0], frame_r.at[n], before).start()

    def arrive(n):
        take(grad_v.at[NF, pl.ds(0, (NR, 2, NR - 2)[n])], frame_r.at[n])

    reduce_start(0, stacked(one, two))
    halo[0].start()
    halo[1].start()
    frame_send(0, 0, half, 0)

    copy_cot.wait()

    def bias_local(i, carry):
        return carry + fold(grad_v[i // NR, 1 + i % NR].astype(F32))

    bias = lax.fori_loop(0, NF * NR, bias_local, zero8, unroll=2)

    def clear_rows(frames):
        @pl.when(slab == 0)
        def _():
            for f in frames:
                grad_v[f, 0] = jnp.zeros((W, C), BF16)

        @pl.when(slab == 15)
        def _():
            for f in frames:
                grad_v[f, NR + 1] = jnp.zeros((W, C), BF16)

    def shifted_sum(o):
        o = o.reshape(-1, W, 3 * C)
        pixel = lax.broadcasted_iota(jnp.int32, (1, W, C), 1)
        left = pltpu.roll(o[:, :, :C], W - 1, 1)
        right = pltpu.roll(o[:, :, 2 * C :], 1, 1)
        return o[:, :, C : 2 * C] + jnp.where(pixel < W - 1, left, 0.0) + jnp.where(pixel > 0, right, 0.0)

    def act_grad(t, taps, add, parts=((0, 4), (4, 4))):
        rhs = jnp.concatenate([w_v[a * 3 + b] for a in taps for b in range(3)], axis=1)
        for r, n in parts:
            lhs = jnp.concatenate(
                [
                    grad_v[t + 2 - a, r + 2 - b : r + 2 - b + n].reshape(n * W, C)
                    for a in taps
                    for b in range(3)
                ],
                axis=1,
            )
            o = shifted_sum(lax.dot_general(lhs, rhs, NT_DIMS, preferred_element_type=F32))
            if add:
                o = o + ag_v[t, r : r + n]
            ag_v[t, r : r + n] = o

    inner, outer = ((2, 4),), ((0, 2), (6, 2))
    first, second = ((0, 4),), ((4, 4),)
    copy_w.wait()
    act_grad(0, (2, 1, 0), False, inner)
    act_grad(1, (2, 1, 0), False, inner)
    act_grad(2, (2, 1), False, inner)
    reduce_middle(0)
    frame_send(0, half, half, 0)
    frame_send(1, 0, 1, 1)
    frame_send(1, NR - 1, 1, 1)
    frame_send(1, 1, NR - 2, 2)
    halo[0].wait_recv()
    halo[1].wait_recv()
    clear_rows(range(NF))
    act_grad(0, (2, 1, 0), False, outer)
    act_grad(1, (2, 1, 0), False, outer)
    act_grad(2, (2, 1), False, outer)
    act_grad(3, (2,), False)
    sums = group_sum(reduce_end(0))
    mean = sums[0:1] / MEMBERS
    variance = sums[1:2] / MEMBERS - mean * mean
    inv = lax.rsqrt(variance + 1e-06)
    gain, shift = gain_ref[...], shift_ref[...]

    pixel = lax.broadcasted_iota(jnp.int32, (C, W), 1)

    def activate(t):
        for r in range(NR):
            normed = (act_v[t, r].astype(F32) - mean) * inv
            scaled = normed * gain + shift
            sigma = jax.nn.sigmoid(scaled)
            dv_v[t, r] = sigma * (1.0 + scaled * (1.0 - sigma))
            turned = (scaled * sigma).T
            at_v[t, r, 0:C] = jnp.where(pixel > 0, pltpu.roll(turned, 1, 1), 0.0).astype(BF16)
            at_v[t, r, C : 2 * C] = turned.astype(BF16)
            at_v[t, r, 2 * C : 3 * C] = jnp.where(pixel < W - 1, pltpu.roll(turned, W - 1, 1), 0.0).astype(BF16)

    def weight_part(a, t):
        lhs = jnp.concatenate([at_v[t, r] for r in range(NR)], axis=1)
        rhs = jnp.concatenate(
            [grad_v[t + 2 - a, 2 - b : 2 - b + NR].reshape(ROWS, C) for b in range(3)], axis=1
        )
        o = jnp.dot(lhs, rhs, preferred_element_type=F32)
        for b in range(3):
            v = o[:, b * C : (b + 1) * C].reshape(3, C, C)
            at = pl.ds((2 - a) * 3, 3)
            wacc[b, at] = v + wacc[b, at] if t else v

    half0 = core * 64
    twin = chip(z, y, x, 1 - core)
    place = (x, y, z)
    groups = ((0, 3), (3, 6), (6, 9))

    def on_axis(b, k):
        return (chip(z, y, k), chip(z, k, x), chip(k, y, x))[b]

    def span_of(start, size):
        return pl.ds(pl.multiple_of(start, 16), size)

    def core_send(g):
        at = pl.ds(3 * g, 3)
        src = wacc.at[:, at, span_of(64 - half0, 64)]
        remote(src, rs_core.at[:, at], send_sem.at[0], c_r.at[g], twin).start()

    def axis_send(g):
        at = pl.ds(3 * g, 3)
        take(rs_core.at[:, at], c_r.at[g])
        here = span_of(half0, 64)
        for b in range(3):
            wacc[b, at, here] = wacc[b, at, here] + rs_core[b, at]
            for d in range(1, 4):
                k = (place[b] + d) % 4
                src = wacc.at[b, at, span_of(half0 + k * 16, 16)]
                to = rs_axis.at[0, b, place[b], at]
                remote(src, to, send_sem.at[0], x_r.at[g, b], on_axis(b, k)).start()

    def mine(b):
        return span_of(half0 + place[b] * 16, 16)

    def exchange(k, g, b, value, recv):
        lo, hi = groups[g]
        axis = (b + k) % 3
        slot = rs_axis.at[k, b, place[axis], pl.ds(lo, hi - lo)]
        slot[...] = value
        for d in range(1, 4):
            remote(slot, slot, send_sem.at[0], recv.at[g, b], on_axis(axis, (place[axis] + d) % 4)).start()

    def along_second(g, b):
        lo, hi = groups[g]
        take(rs_axis.at[0, b, pl.ds(0, 3), pl.ds(lo, 3)], x_r.at[g, b])
        rs_axis[0, b, place[b], pl.ds(lo, hi - lo)] = wacc[b, lo:hi, mine(b)]
        exchange(1, g, b, rs_axis[0, b, :, lo:hi].sum(axis=0), y_r)

    def along_third(g, b):
        lo, hi = groups[g]
        take(rs_axis.at[1, b, pl.ds(0, 3), pl.ds(lo, hi - lo)], y_r.at[g, b])
        exchange(2, g, b, rs_axis[1, b, :, lo:hi].sum(axis=0), z_r)

    def gather_axis(g, b):
        lo, hi = groups[g]
        take(rs_axis.at[2, b, pl.ds(0, 3), pl.ds(lo, hi - lo)], z_r.at[g, b])
        total = rs_axis[2, b, :, lo:hi].sum(axis=0) * SCALE
        wout[b, lo:hi, mine(b)] = total.astype(BF16)
        tiles = wout.at[b, pl.ds(lo, hi - lo), mine(b)]
        for d in range(1, 4):
            remote(tiles, tiles, send_sem.at[0], gx_r.at[g, b], on_axis(b, (place[b] + d) % 4)).start()

    def gather_core(g, b):
        lo, hi = groups[g]
        take(wout.at[b, pl.ds(lo, hi - lo), pl.ds(0, 48)], gx_r.at[g, b])
        part = wout.at[b, pl.ds(lo, hi - lo), span_of(half0, 64)]
        remote(part, part, send_sem.at[0], gc_r.at[g, b], twin).start()

    def complete(g, b):
        lo, hi = groups[g]
        take(wout.at[b, pl.ds(lo, hi - lo), pl.ds(0, 64)], gc_r.at[g, b])
        for j in range(lo, hi, 3):
            wide[2 - j // 3, b] = wout[b, j : j + 3].astype(F32)

    def each(stage, g):
        for b in range(3):
            stage(g, b)

    def clear_frame(f):
        @pl.when(span == 7)
        def _():
            def clear(i, _):
                grad_v[f, i] = jnp.zeros((W, C), BF16)
                return 0

            lax.fori_loop(0, NR + 2, clear, 0)

    def outer_rows(n, f):
        halo[n].wait_recv()
        halo[n].wait_send()
        halo[n + 1].wait_recv()
        halo[n + 1].wait_send()
        clear_rows((f,))
        clear_frame(f)

    activate(0)
    weight_part(2, 0)
    activate(1)
    weight_part(2, 1)
    activate(2)
    arrive(0)
    halo[2].start()
    halo[3].start()
    weight_part(2, 2)
    activate(3)
    arrive(1)
    halo[4].start()
    halo[5].start()
    weight_part(2, 3)
    core_send(0)
    for t in range(3):
        weight_part(1, t)
    outer_rows(2, NF)
    axis_send(0)
    weight_part(1, 3)
    core_send(1)
    for t in range(3):
        weight_part(0, t)
    arrive(2)
    outer_rows(4, NF + 1)
    axis_send(1)
    weight_part(0, 3)
    core_send(2)
    act_grad(3, (1, 0), True)
    axis_send(2)
    each(along_second, 0)
    act_grad(2, (0,), True)

    def finish(i, carry):
        t, r = i // NR, i % NR
        normed = (act_v[t, r].astype(F32) - mean) * inv
        pre = ag_v[t, r] * dv_v[t, r]
        ag_v[t, r] = pre
        return carry[0] + fold(pre * normed), carry[1] + fold(pre)

    gain_sum, shift_sum = lax.fori_loop(0, NF * NR, finish, (zero8, zero8), unroll=2)
    reduce_start(1, stacked(gain_sum, shift_sum, bias))
    each(along_second, 1)
    each(along_second, 2)
    reduce_middle(1)
    each(along_third, 0)
    each(along_third, 1)
    each(along_third, 2)
    each(gather_axis, 0)
    each(gather_axis, 1)
    total = reduce_end(1)
    sums_ref[...] = total * SCALE
    means = group_sum(total * gain) / MEMBERS
    mean_two, mean_one = means[0:1], means[1:2]

    def result(i, _):
        t, r = i // NR, i % NR
        normed = (act_v[t, r].astype(F32) - mean) * inv
        outb[t, r] = (inv * (gain * ag_v[t, r] - mean_one - normed * mean_two)).astype(BF16)
        return 0

    lax.fori_loop(0, NF * NR, result, 0, unroll=2)
    each(gather_axis, 2)
    for g in range(GROUPS):
        each(gather_core, g)
    for g in range(GROUPS):
        each(complete, g)
    sent(all_sent, send_sem.at[0])


def write_out(in_ref, w_ref, sums_ref, out_hbm, wout_hbm, gain_ref, shift_ref, bias_ref, sem):
    copies = [pltpu.make_async_copy(w_ref.at[a], wout_hbm.at[a], sem.at[a]) for a in range(3)]
    copies.append(pltpu.make_async_copy(in_ref, out_hbm, sem.at[3]))
    for copy in copies:
        copy.start()
    gain_ref[...] = sums_ref[0:1]
    shift_ref[...] = sums_ref[1:2]
    bias_ref[...] = sums_ref[2:3]
    for copy in copies:
        copy.wait()


def body(activations, cotangent, conv_weight, norm_gain, norm_shift):
    anywhere = pl.BlockSpec(memory_space=pl.ANY)
    vmem = pl.BlockSpec(memory_space=pltpu.VMEM)
    dma = pltpu.SemaphoreType.DMA
    input_grad, weights, sums = pl.pallas_call(
        kernel,
        out_shape=(
            pltpu.VMEM((NF, NR, W, C), BF16),
            pltpu.VMEM((3, 3, 3, C, C), F32),
            pltpu.VMEM((4, C), F32),
        ),
        in_specs=[anywhere, anywhere, anywhere, vmem, vmem],
        out_specs=(vmem, vmem, vmem),
        scratch_shapes=[
            pltpu.VMEM((NF, NR, W, C), BF16),
            pltpu.VMEM((NF + 2, NR + 2, W, C), BF16),
            pltpu.VMEM((9, 3 * C, C), BF16),
            pltpu.VMEM((NF, NR, 3 * C, W), BF16),
            pltpu.VMEM((NF, NR, W, C), F32),
            pltpu.VMEM((NF, NR, W, C), F32),
            pltpu.VMEM((3, 9, C, C), F32),
            pltpu.VMEM((3, 9, 64, C), F32),
            pltpu.VMEM((3, 3, 4, 9, 16, C), F32),
            pltpu.VMEM((3, 9, C, C), BF16),
            pltpu.VMEM((2, 2, 4, C), F32),
            pltpu.VMEM((2, 16, 4, C), F32),
            pltpu.VMEM((2, 8, 4, C), F32),
            pltpu.VMEM((SENT, C), F32),
            dma((6,)), dma((5,)), dma((6,)), dma((3,)), dma((2, 2)), dma((3,)), dma((3, 3)),
            dma((GROUPS, 3)), dma((GROUPS, 3)), dma((GROUPS, 3)), dma((GROUPS, 3)),
        ],
        compiler_params=pltpu.CompilerParams(
            collective_id=0, has_side_effects=True, vmem_limit_bytes=64_100_000
        ),
    )(
        activations,
        cotangent,
        conv_weight.reshape(9, 3 * C, C),
        norm_gain.reshape(1, C),
        norm_shift.reshape(1, C),
    )
    per_channel = jax.ShapeDtypeStruct((1, C), F32)
    input_grad, weight_grad, gain_grad, shift_grad, bias_grad = pl.pallas_call(
        write_out,
        out_shape=(
            jax.ShapeDtypeStruct((NF, NR, W, C), BF16),
            jax.ShapeDtypeStruct((3, 3, 3, C, C), F32),
            per_channel,
            per_channel,
            per_channel,
        ),
        in_specs=[vmem, vmem, vmem],
        out_specs=(anywhere, anywhere, vmem, vmem, vmem),
        scratch_shapes=[dma((4,))],
        compiler_params=pltpu.CompilerParams(vmem_limit_bytes=16 * 1024 * 1024),
    )(input_grad, weights, sums)
    return input_grad, weight_grad, gain_grad.reshape(C), shift_grad.reshape(C), bias_grad.reshape(C)


def solution(mesh):
    placed = (P("span", "slab", None, None), P("span", "slab", None, None), P(), P(), P())
    return jax.shard_map(
        body,
        mesh=mesh,
        in_specs=placed,
        out_specs=(P("span", "slab", None, None), P(), P(), P(), P()),
        check_vma=False,
    )
```

```python
import jax
import jax.numpy as jnp
from jax import lax
from jax.experimental import pallas as pl
from jax.experimental.pallas import tpu as pltpu
from jax.sharding import PartitionSpec as P

MESH = pl.DeviceIdType.MESH
F32 = jnp.float32
BF16 = jnp.bfloat16
NF, NR, W, C = 4, 8, 128, 128
ROWS = NR * W
CELLS = 32 * 128 * 128
MEMBERS = CELLS * 4
SCALE = float(CELLS) ** -0.5
SENT = 2 * NF * 64 + 2 * NR * 64 + 2 * (7 + 15) * 4 + 27 * 64 + 3 * 27 * 48 + 18 * 24 + 18 * 32 + 9 * 56
GROUPS = 3
NT_DIMS = (((1,), (1,)), ((), ()))


def group_sum(v):
    lane = lax.broadcasted_iota(jnp.int32, v.shape, 1)
    v = v + jnp.where(lane % 2 == 0, pltpu.roll(v, C - 1, 1), pltpu.roll(v, 1, 1))
    return v + jnp.where(lane % 4 < 2, pltpu.roll(v, C - 2, 1), pltpu.roll(v, 2, 1))


def fold(v):
    return v.reshape(-1, 8, C).sum(axis=0)


def kernel(
    act_hbm, cot_hbm, w_hbm, gain_ref, shift_ref,
    outb, wide, sums_ref,
    act_v, grad_v, w_v, at_v, ag_v, dv_v, wacc, rs_core, rs_axis, wout, stat, arb, ara,
    all_sent, loc_sem, send_sem, halo_r, frame_r, ar_r, c_r, x_r, y_r, z_r, gx_r, gc_r,
):
    span, slab = lax.axis_index("span"), lax.axis_index("slab")
    z, y = span // 2, (span % 2) * 2 + slab // 8
    xc = slab % 8
    x, core = xc // 2, xc % 2

    def chip(cz, cy, cx, cc=core):
        return (cz * 2 + cy // 2, (cy % 2) * 8 + cx * 2 + cc)

    barrier = pltpu.get_barrier_semaphore()
    above = (span, (slab + 15) % 16)
    below = (span, (slab + 1) % 16)
    greeted = [chip(z, y, (x + d // 2) % 4, (core + d) % 2) for d in range(1, 8)]
    greeted += [above, below]
    greeted += [chip((z + d // 4) % 4, (y + d % 4) % 4, x) for d in range(1, 16)]
    greeted += [chip(z, (y + d) % 4, x, 1 - core) for d in range(1, 4)]
    greeted += [chip((z + d) % 4, y, x, 1 - core) for d in range(1, 4)]

    def greet(devices):
        for device in devices:
            pl.semaphore_signal(barrier, inc=1, device_id=device, device_id_type=MESH)

    greet(greeted[:7])
    copies_act = [pltpu.make_async_copy(act_hbm.at[t], act_v.at[t], loc_sem.at[t]) for t in range(NF)]
    copy_cot = pltpu.make_async_copy(cot_hbm, grad_v.at[pl.ds(0, NF), pl.ds(1, NR)], loc_sem.at[NF])
    copy_w = pltpu.make_async_copy(w_hbm, w_v, loc_sem.at[NF + 1])
    for copy in copies_act:
        copy.start()
    copy_cot.start()
    copy_w.start()
    greet(greeted[7:])

    def remote(src, dst, send, recv, device):
        return pltpu.make_async_remote_copy(
            src_ref=src, dst_ref=dst, send_sem=send, recv_sem=recv, device_id=device, device_id_type=MESH
        )

    def take(ref, recv):
        remote(ref, ref, recv, recv, below).wait_recv()

    def sent(ref, send):
        remote(ref, ref, send, send, below).wait_send()

    zero8 = jnp.zeros((8, C), F32)
    one, two = zero8, zero8
    for t in range(NF):
        copies_act[t].wait()

        def local_sums(r, carry, t=t):
            v = act_v[t, r].astype(F32)
            return carry[0] + fold(v), carry[1] + fold(v * v)

        one, two = lax.fori_loop(0, NR, local_sums, (one, two), unroll=2)
    row = lax.broadcasted_iota(jnp.int32, (4, C), 0)

    def stacked(*sums):
        value = jnp.zeros((4, C), F32)
        for n, v in enumerate(sums):
            value = jnp.where(row == n, jnp.broadcast_to(v.sum(axis=0, keepdims=True), (4, C)), value)
        return value

    def in_yz(q):
        return chip(q // 4, q % 4, x)

    def in_row(j):
        return chip(z, y, j // 2, j % 2)

    yz = z * 4 + y

    def reduce_start(n, value):
        stat[n, 0] = value
        ara[n, xc] = value
        for d in range(1, 8):
            remote(stat.at[n, 0], ara.at[n, xc], send_sem.at[0], ar_r.at[n, 0], in_row((xc + d) % 8)).start()

    def reduce_middle(n):
        take(ara.at[n, pl.ds(0, 7)], ar_r.at[n, 0])
        value = ara[n].sum(axis=0)
        stat[n, 1] = value
        arb[n, yz] = value
        for d in range(1, 16):
            remote(stat.at[n, 1], arb.at[n, yz], send_sem.at[0], ar_r.at[n, 1], in_yz((yz + d) % 16)).start()

    def reduce_end(n):
        take(arb.at[n, pl.ds(0, 15)], ar_r.at[n, 1])
        return arb[n].sum(axis=0)

    pl.semaphore_wait(barrier, len(greeted))

    halo = [
        remote(cot_hbm.at[:, 0], grad_v.at[pl.ds(0, NF), NR + 1], send_sem.at[0], halo_r.at[0], above),
        remote(cot_hbm.at[:, NR - 1], grad_v.at[pl.ds(0, NF), 0], send_sem.at[0], halo_r.at[1], below),
        remote(grad_v.at[NF, 1], grad_v.at[NF, NR + 1], send_sem.at[1], halo_r.at[2], above),
        remote(grad_v.at[NF, NR], grad_v.at[NF, 0], send_sem.at[2], halo_r.at[3], below),
        remote(grad_v.at[NF + 1, 1], grad_v.at[NF + 1, NR + 1], send_sem.at[3], halo_r.at[4], above),
        remote(grad_v.at[NF + 1, NR], grad_v.at[NF + 1, 0], send_sem.at[4], halo_r.at[5], below),
    ]
    before = ((span + 7) % 8, slab)
    half = NR // 2

    def frame_send(f, start, size, n):
        to = grad_v.at[NF + f, pl.ds(1 + start, size)]
        remote(cot_hbm.at[f, pl.ds(start, size)], to, send_sem.at[0], frame_r.at[n], before).start()

    def arrive(n):
        take(grad_v.at[NF, pl.ds(0, (NR, 2, NR - 2)[n])], frame_r.at[n])

    reduce_start(0, stacked(one, two))
    halo[0].start()
    halo[1].start()
    frame_send(0, 0, half, 0)

    copy_cot.wait()

    def bias_local(i, carry):
        return carry + fold(grad_v[i // NR, 1 + i % NR].astype(F32))

    bias = lax.fori_loop(0, NF * NR, bias_local, zero8, unroll=2)

    def clear_rows(frames):
        @pl.when(slab == 0)
        def _():
            for f in frames:
                grad_v[f, 0] = jnp.zeros((W, C), BF16)

        @pl.when(slab == 15)
        def _():
            for f in frames:
                grad_v[f, NR + 1] = jnp.zeros((W, C), BF16)

    def shifted_sum(o):
        o = o.reshape(-1, W, 3 * C)
        pixel = lax.broadcasted_iota(jnp.int32, (1, W, C), 1)
        left = pltpu.roll(o[:, :, :C], W - 1, 1)
        right = pltpu.roll(o[:, :, 2 * C :], 1, 1)
        return o[:, :, C : 2 * C] + jnp.where(pixel < W - 1, left, 0.0) + jnp.where(pixel > 0, right, 0.0)

    def act_grad(t, taps, add, parts=((0, 4), (4, 4))):
        rhs = jnp.concatenate([w_v[a * 3 + b] for a in taps for b in range(3)], axis=1)
        for r, n in parts:
            lhs = jnp.concatenate(
                [
                    grad_v[t + 2 - a, r + 2 - b : r + 2 - b + n].reshape(n * W, C)
                    for a in taps
                    for b in range(3)
                ],
                axis=1,
            )
            o = shifted_sum(lax.dot_general(lhs, rhs, NT_DIMS, preferred_element_type=F32))
            if add:
                o = o + ag_v[t, r : r + n]
            ag_v[t, r : r + n] = o

    inner, outer = ((2, 4),), ((0, 2), (6, 2))
    first, second = ((0, 4),), ((4, 4),)
    copy_w.wait()
    act_grad(0, (2, 1, 0), False, inner)
    act_grad(1, (2, 1, 0), False, inner)
    act_grad(2, (2, 1), False, inner)
    reduce_middle(0)
    frame_send(0, half, half, 0)
    frame_send(1, 0, 1, 1)
    frame_send(1, NR - 1, 1, 1)
    frame_send(1, 1, NR - 2, 2)
    halo[0].wait_recv()
    halo[1].wait_recv()
    clear_rows(range(NF))
    act_grad(0, (2, 1, 0), False, outer)
    act_grad(1, (2, 1, 0), False, outer)
    act_grad(2, (2, 1), False, outer)
    act_grad(3, (2,), False)
    sums = group_sum(reduce_end(0))
    mean = sums[0:1] / MEMBERS
    variance = sums[1:2] / MEMBERS - mean * mean
    inv = lax.rsqrt(variance + 1e-06)
    gain, shift = gain_ref[...], shift_ref[...]

    pixel = lax.broadcasted_iota(jnp.int32, (C, W), 1)

    def activate(t):
        for r in range(NR):
            normed = (act_v[t, r].astype(F32) - mean) * inv
            scaled = normed * gain + shift
            sigma = jax.nn.sigmoid(scaled)
            dv_v[t, r] = sigma * (1.0 + scaled * (1.0 - sigma))
            turned = (scaled * sigma).T
            at_v[t, r, 0:C] = jnp.where(pixel > 0, pltpu.roll(turned, 1, 1), 0.0).astype(BF16)
            at_v[t, r, C : 2 * C] = turned.astype(BF16)
            at_v[t, r, 2 * C : 3 * C] = jnp.where(pixel < W - 1, pltpu.roll(turned, W - 1, 1), 0.0).astype(BF16)

    def weight_part(a, t):
        lhs = jnp.concatenate([at_v[t, r] for r in range(NR)], axis=1)
        rhs = jnp.concatenate(
            [grad_v[t + 2 - a, 2 - b : 2 - b + NR].reshape(ROWS, C) for b in range(3)], axis=1
        )
        o = jnp.dot(lhs, rhs, preferred_element_type=F32)
        for b in range(3):
            v = o[:, b * C : (b + 1) * C].reshape(3, C, C)
            at = pl.ds((2 - a) * 3, 3)
            wacc[b, at] = v + wacc[b, at] if t else v

    half0 = core * 64
    twin = chip(z, y, x, 1 - core)
    place = (x, y, z)
    groups = ((0, 3), (3, 6), (6, 9))

    def on_axis(b, k, cc=core):
        return (chip(z, y, k, cc), chip(z, k, x, cc), chip(k, y, x, cc))[b]

    def span_of(start, size):
        return pl.ds(pl.multiple_of(start, 16), size)

    def core_send(g):
        at = pl.ds(3 * g, 3)
        src = wacc.at[:, at, span_of(64 - half0, 64)]
        remote(src, rs_core.at[:, at], send_sem.at[0], c_r.at[g], twin).start()

    def axis_send(g):
        at = pl.ds(3 * g, 3)
        take(rs_core.at[:, at], c_r.at[g])
        here = span_of(half0, 64)
        for b in range(3):
            wacc[b, at, here] = wacc[b, at, here] + rs_core[b, at]
            for d in range(1, 4):
                k = (place[b] + d) % 4
                src = wacc.at[b, at, span_of(half0 + k * 16, 16)]
                to = rs_axis.at[0, b, place[b], at]
                remote(src, to, send_sem.at[0], x_r.at[g, b], on_axis(b, k)).start()

    def mine(b):
        return span_of(half0 + place[b] * 16, 16)

    def exchange(k, g, b, value, recv):
        lo, hi = groups[g]
        axis = (b + k) % 3
        slot = rs_axis.at[k, b, place[axis], pl.ds(lo, hi - lo)]
        slot[...] = value
        for d in range(1, 4):
            remote(slot, slot, send_sem.at[0], recv.at[g, b], on_axis(axis, (place[axis] + d) % 4)).start()

    def along_second(g, b):
        lo, hi = groups[g]
        take(rs_axis.at[0, b, pl.ds(0, 3), pl.ds(lo, 3)], x_r.at[g, b])
        rs_axis[0, b, place[b], pl.ds(lo, hi - lo)] = wacc[b, lo:hi, mine(b)]
        exchange(1, g, b, rs_axis[0, b, :, lo:hi].sum(axis=0), y_r)

    def along_third(g, b):
        lo, hi = groups[g]
        take(rs_axis.at[1, b, pl.ds(0, 3), pl.ds(lo, hi - lo)], y_r.at[g, b])
        exchange(2, g, b, rs_axis[1, b, :, lo:hi].sum(axis=0), z_r)

    def gather_axis(g, b):
        lo, hi = groups[g]
        take(rs_axis.at[2, b, pl.ds(0, 3), pl.ds(lo, hi - lo)], z_r.at[g, b])
        total = rs_axis[2, b, :, lo:hi].sum(axis=0) * SCALE
        wout[b, lo:hi, mine(b)] = total.astype(BF16)
        tiles = wout.at[b, pl.ds(lo, hi - lo), mine(b)]
        for d in range(1, 8) if g == 2 else (2, 4, 6):
            to = on_axis(b, (place[b] + d // 2) % 4, (core + d) % 2)
            remote(tiles, tiles, send_sem.at[0], gx_r.at[g, b], to).start()

    def gather_core(g, b):
        lo, hi = groups[g]
        take(wout.at[b, pl.ds(lo, hi - lo), pl.ds(0, 48)], gx_r.at[g, b])
        part = wout.at[b, pl.ds(lo, hi - lo), span_of(half0, 64)]
        remote(part, part, send_sem.at[0], gc_r.at[g, b], twin).start()

    def complete(g, b):
        lo, hi = groups[g]
        if g == 2:
            take(wout.at[b, pl.ds(lo, hi - lo), pl.ds(0, 112)], gx_r.at[g, b])
        else:
            take(wout.at[b, pl.ds(lo, hi - lo), pl.ds(0, 64)], gc_r.at[g, b])
        wide[2 - g, b] = wout[b, lo:hi].astype(F32)

    def each(stage, g):
        for b in range(3):
            stage(g, b)

    def clear_frame(f):
        @pl.when(span == 7)
        def _():
            def clear(i, _):
                grad_v[f, i] = jnp.zeros((W, C), BF16)
                return 0

            lax.fori_loop(0, NR + 2, clear, 0)

    def outer_rows(n, f):
        halo[n].wait_recv()
        halo[n].wait_send()
        halo[n + 1].wait_recv()
        halo[n + 1].wait_send()
        clear_rows((f,))
        clear_frame(f)

    activate(0)
    weight_part(2, 0)
    activate(1)
    weight_part(2, 1)
    activate(2)
    arrive(0)
    halo[2].start()
    halo[3].start()
    weight_part(2, 2)
    activate(3)
    arrive(1)
    halo[4].start()
    halo[5].start()
    weight_part(2, 3)
    core_send(0)
    for t in range(3):
        weight_part(1, t)
    for t in range(2):
        weight_part(0, t)
    axis_send(0)
    outer_rows(2, NF)
    weight_part(1, 3)
    core_send(1)
    weight_part(0, 2)
    arrive(2)
    outer_rows(4, NF + 1)
    weight_part(0, 3)
    core_send(2)
    axis_send(1)
    act_grad(3, (1, 0), True)
    axis_send(2)
    each(along_second, 0)
    act_grad(2, (0,), True)

    def finish(i, carry):
        t, r = i // NR, i % NR
        normed = (act_v[t, r].astype(F32) - mean) * inv
        pre = ag_v[t, r] * dv_v[t, r]
        ag_v[t, r] = pre
        return carry[0] + fold(pre * normed), carry[1] + fold(pre)

    gain_sum, shift_sum = lax.fori_loop(0, NF * NR, finish, (zero8, zero8), unroll=2)
    reduce_start(1, stacked(gain_sum, shift_sum, bias))
    each(along_second, 1)
    each(along_second, 2)
    each(along_third, 0)
    each(along_third, 1)
    reduce_middle(1)
    each(along_third, 2)
    each(gather_axis, 0)
    each(gather_axis, 1)
    each(gather_axis, 2)
    total = reduce_end(1)
    sums_ref[...] = total * SCALE
    means = group_sum(total * gain) / MEMBERS
    mean_two, mean_one = means[0:1], means[1:2]

    def result(i, _):
        t, r = i // NR, i % NR
        normed = (act_v[t, r].astype(F32) - mean) * inv
        outb[t, r] = (inv * (gain * ag_v[t, r] - mean_one - normed * mean_two)).astype(BF16)
        return 0

    lax.fori_loop(0, NF * NR, result, 0, unroll=2)
    each(gather_core, 0)
    each(gather_core, 1)
    for g in range(GROUPS):
        each(complete, g)
    sent(all_sent, send_sem.at[0])


def write_out(in_ref, w_ref, sums_ref, out_hbm, wout_hbm, gain_ref, shift_ref, bias_ref, sem):
    copies = [pltpu.make_async_copy(w_ref.at[a], wout_hbm.at[a], sem.at[a]) for a in range(3)]
    copies.append(pltpu.make_async_copy(in_ref, out_hbm, sem.at[3]))
    for copy in copies:
        copy.start()
    gain_ref[...] = sums_ref[0:1]
    shift_ref[...] = sums_ref[1:2]
    bias_ref[...] = sums_ref[2:3]
    for copy in copies:
        copy.wait()


def body(activations, cotangent, conv_weight, norm_gain, norm_shift):
    anywhere = pl.BlockSpec(memory_space=pl.ANY)
    vmem = pl.BlockSpec(memory_space=pltpu.VMEM)
    dma = pltpu.SemaphoreType.DMA
    input_grad, weights, sums = pl.pallas_call(
        kernel,
        out_shape=(
            pltpu.VMEM((NF, NR, W, C), BF16),
            pltpu.VMEM((3, 3, 3, C, C), F32),
            pltpu.VMEM((4, C), F32),
        ),
        in_specs=[anywhere, anywhere, anywhere, vmem, vmem],
        out_specs=(vmem, vmem, vmem),
        scratch_shapes=[
            pltpu.VMEM((NF, NR, W, C), BF16),
            pltpu.VMEM((NF + 2, NR + 2, W, C), BF16),
            pltpu.VMEM((9, 3 * C, C), BF16),
            pltpu.VMEM((NF, NR, 3 * C, W), BF16),
            pltpu.VMEM((NF, NR, W, C), F32),
            pltpu.VMEM((NF, NR, W, C), F32),
            pltpu.VMEM((3, 9, C, C), F32),
            pltpu.VMEM((3, 9, 64, C), F32),
            pltpu.VMEM((3, 3, 4, 9, 16, C), F32),
            pltpu.VMEM((3, 9, C, C), BF16),
            pltpu.VMEM((2, 2, 4, C), F32),
            pltpu.VMEM((2, 16, 4, C), F32),
            pltpu.VMEM((2, 8, 4, C), F32),
            pltpu.VMEM((SENT, C), F32),
            dma((6,)), dma((5,)), dma((6,)), dma((3,)), dma((2, 2)), dma((3,)), dma((3, 3)),
            dma((GROUPS, 3)), dma((GROUPS, 3)), dma((GROUPS, 3)), dma((2, 3)),
        ],
        compiler_params=pltpu.CompilerParams(
            collective_id=0, has_side_effects=True, vmem_limit_bytes=64_100_000
        ),
    )(
        activations,
        cotangent,
        conv_weight.reshape(9, 3 * C, C),
        norm_gain.reshape(1, C),
        norm_shift.reshape(1, C),
    )
    per_channel = jax.ShapeDtypeStruct((1, C), F32)
    input_grad, weight_grad, gain_grad, shift_grad, bias_grad = pl.pallas_call(
        write_out,
        out_shape=(
            jax.ShapeDtypeStruct((NF, NR, W, C), BF16),
            jax.ShapeDtypeStruct((3, 3, 3, C, C), F32),
            per_channel,
            per_channel,
            per_channel,
        ),
        in_specs=[vmem, vmem, vmem],
        out_specs=(anywhere, anywhere, vmem, vmem, vmem),
        scratch_shapes=[dma((4,))],
        compiler_params=pltpu.CompilerParams(vmem_limit_bytes=16 * 1024 * 1024),
    )(input_grad, weights, sums)
    return input_grad, weight_grad, gain_grad.reshape(C), shift_grad.reshape(C), bias_grad.reshape(C)


def solution(mesh):
    placed = (P("span", "slab", None, None), P("span", "slab", None, None), P(), P(), P())
    return jax.shard_map(
        body,
        mesh=mesh,
        in_specs=placed,
        out_specs=(P("span", "slab", None, None), P(), P(), P(), P()),
        check_vma=False,
    )
```

```python
import jax
import jax.numpy as jnp
from jax import lax
from jax.experimental import pallas as pl
from jax.experimental.pallas import tpu as pltpu
from jax.sharding import PartitionSpec as P

MESH = pl.DeviceIdType.MESH
F32 = jnp.float32
BF16 = jnp.bfloat16
NF, NR, W, C = 4, 8, 128, 128
ROWS = NR * W
CELLS = 32 * 128 * 128
MEMBERS = CELLS * 4
SCALE = float(CELLS) ** -0.5
SENT = 2 * NF * 64 + 2 * NR * 64 + 2 * (7 + 15) * 4 + 27 * 64 + 3 * 27 * 48 + 18 * 24 + 18 * 32 + 9 * 56
GROUPS = 3
NT_DIMS = (((1,), (1,)), ((), ()))


def group_sum(v):
    lane = lax.broadcasted_iota(jnp.int32, v.shape, 1)
    v = v + jnp.where(lane % 2 == 0, pltpu.roll(v, C - 1, 1), pltpu.roll(v, 1, 1))
    return v + jnp.where(lane % 4 < 2, pltpu.roll(v, C - 2, 1), pltpu.roll(v, 2, 1))


def fold(v):
    return v.reshape(-1, 8, C).sum(axis=0)


def kernel(
    act_hbm, cot_hbm, w_hbm, gain_hbm, shift_hbm,
    outb, wide, gain_out, shift_out, bias_out,
    gain_v, shift_v, act_v, grad_v, w_v, at_v, ag_v, dv_v, wacc, rs_core, rs_axis, wout, stat, arb, ara,
    all_sent, loc_sem, send_sem, halo_r, frame_r, ar_r, c_r, x_r, y_r, z_r, gx_r, gc_r,
):
    span, slab = lax.axis_index("span"), lax.axis_index("slab")
    z, y = span // 2, (span % 2) * 2 + slab // 8
    xc = slab % 8
    x, core = xc // 2, xc % 2

    def chip(cz, cy, cx, cc=core):
        return (cz * 2 + cy // 2, (cy % 2) * 8 + cx * 2 + cc)

    barrier = pltpu.get_barrier_semaphore()
    above = (span, (slab + 15) % 16)
    below = (span, (slab + 1) % 16)
    greeted = [chip(z, y, (x + d // 2) % 4, (core + d) % 2) for d in range(1, 8)]
    greeted += [above, below]
    greeted += [chip((z + d // 4) % 4, (y + d % 4) % 4, x) for d in range(1, 16)]
    greeted += [chip(z, (y + d) % 4, x, 1 - core) for d in range(1, 4)]
    greeted += [chip((z + d) % 4, y, x, 1 - core) for d in range(1, 4)]

    def greet(devices):
        for device in devices:
            pl.semaphore_signal(barrier, inc=1, device_id=device, device_id_type=MESH)

    greet(greeted[:7])
    copies_act = [pltpu.make_async_copy(act_hbm.at[t], act_v.at[t], loc_sem.at[t]) for t in range(NF)]
    copy_cot = pltpu.make_async_copy(cot_hbm, grad_v.at[pl.ds(0, NF), pl.ds(1, NR)], loc_sem.at[NF])
    copy_w = pltpu.make_async_copy(w_hbm, w_v, loc_sem.at[NF + 1])
    copy_gain = pltpu.make_async_copy(gain_hbm, gain_v, loc_sem.at[NF + 2])
    copy_shift = pltpu.make_async_copy(shift_hbm, shift_v, loc_sem.at[NF + 3])
    for copy in copies_act:
        copy.start()
    greet(greeted[7:])

    def remote(src, dst, send, recv, device):
        return pltpu.make_async_remote_copy(
            src_ref=src, dst_ref=dst, send_sem=send, recv_sem=recv, device_id=device, device_id_type=MESH
        )

    def take(ref, recv):
        remote(ref, ref, recv, recv, below).wait_recv()

    def sent(ref, send):
        remote(ref, ref, send, send, below).wait_send()

    zero8 = jnp.zeros((8, C), F32)
    one, two = zero8, zero8
    for t in range(NF):
        copies_act[t].wait()
        if t == NF - 2:
            copy_cot.start()
        if t == NF - 1:
            for copy in (copy_w, copy_gain, copy_shift):
                copy.start()

        def local_sums(r, carry, t=t):
            v = act_v[t, r].astype(F32)
            return carry[0] + fold(v), carry[1] + fold(v * v)

        one, two = lax.fori_loop(0, NR, local_sums, (one, two), unroll=2)
    row = lax.broadcasted_iota(jnp.int32, (4, C), 0)

    def stacked(*sums):
        value = jnp.zeros((4, C), F32)
        for n, v in enumerate(sums):
            value = jnp.where(row == n, jnp.broadcast_to(v.sum(axis=0, keepdims=True), (4, C)), value)
        return value

    def in_yz(q):
        return chip(q // 4, q % 4, x)

    def in_row(j):
        return chip(z, y, j // 2, j % 2)

    yz = z * 4 + y

    def reduce_start(n, value):
        stat[n, 0] = value
        ara[n, xc] = value
        for d in range(1, 8):
            remote(stat.at[n, 0], ara.at[n, xc], send_sem.at[0], ar_r.at[n, 0], in_row((xc + d) % 8)).start()

    def reduce_middle(n):
        take(ara.at[n, pl.ds(0, 7)], ar_r.at[n, 0])
        value = ara[n].sum(axis=0)
        stat[n, 1] = value
        arb[n, yz] = value
        for d in range(1, 16):
            remote(stat.at[n, 1], arb.at[n, yz], send_sem.at[0], ar_r.at[n, 1], in_yz((yz + d) % 16)).start()

    def reduce_end(n):
        take(arb.at[n, pl.ds(0, 15)], ar_r.at[n, 1])
        return arb[n].sum(axis=0)

    pl.semaphore_wait(barrier, len(greeted))

    halo = [
        remote(cot_hbm.at[:, 0], grad_v.at[pl.ds(0, NF), NR + 1], send_sem.at[0], halo_r.at[0], above),
        remote(cot_hbm.at[:, NR - 1], grad_v.at[pl.ds(0, NF), 0], send_sem.at[0], halo_r.at[1], below),
        remote(grad_v.at[NF, 1], grad_v.at[NF, NR + 1], send_sem.at[1], halo_r.at[2], above),
        remote(grad_v.at[NF, NR], grad_v.at[NF, 0], send_sem.at[2], halo_r.at[3], below),
        remote(grad_v.at[NF + 1, 1], grad_v.at[NF + 1, NR + 1], send_sem.at[3], halo_r.at[4], above),
        remote(grad_v.at[NF + 1, NR], grad_v.at[NF + 1, 0], send_sem.at[4], halo_r.at[5], below),
    ]
    before = ((span + 7) % 8, slab)
    half = NR // 2

    def frame_send(f, start, size, n):
        to = grad_v.at[NF + f, pl.ds(1 + start, size)]
        remote(cot_hbm.at[f, pl.ds(start, size)], to, send_sem.at[0], frame_r.at[n], before).start()

    def arrive(n):
        take(grad_v.at[NF, pl.ds(0, (NR, 2, NR - 2)[n])], frame_r.at[n])

    reduce_start(0, stacked(one, two))
    halo[0].start()
    halo[1].start()
    frame_send(0, 0, half, 0)

    copy_cot.wait()

    def bias_local(i, carry):
        return carry + fold(grad_v[i // NR, 1 + i % NR].astype(F32))

    bias = lax.fori_loop(0, NF * NR, bias_local, zero8, unroll=2)

    def clear_rows(frames):
        @pl.when(slab == 0)
        def _():
            for f in frames:
                grad_v[f, 0] = jnp.zeros((W, C), BF16)

        @pl.when(slab == 15)
        def _():
            for f in frames:
                grad_v[f, NR + 1] = jnp.zeros((W, C), BF16)

    def shifted_sum(o):
        o = o.reshape(-1, W, 3 * C)
        pixel = lax.broadcasted_iota(jnp.int32, (1, W, C), 1)
        left = pltpu.roll(o[:, :, :C], W - 1, 1)
        right = pltpu.roll(o[:, :, 2 * C :], 1, 1)
        return o[:, :, C : 2 * C] + jnp.where(pixel < W - 1, left, 0.0) + jnp.where(pixel > 0, right, 0.0)

    def act_grad(t, taps, add, parts=((0, 4), (4, 4))):
        rhs = jnp.concatenate([w_v[a * 3 + b] for a in taps for b in range(3)], axis=1)
        for r, n in parts:
            lhs = jnp.concatenate(
                [
                    grad_v[t + 2 - a, r + 2 - b : r + 2 - b + n].reshape(n * W, C)
                    for a in taps
                    for b in range(3)
                ],
                axis=1,
            )
            o = shifted_sum(lax.dot_general(lhs, rhs, NT_DIMS, preferred_element_type=F32))
            if add:
                o = o + ag_v[t, r : r + n]
            ag_v[t, r : r + n] = o

    inner, outer = ((2, 4),), ((0, 2), (6, 2))
    first, second = ((0, 4),), ((4, 4),)
    copy_w.wait()
    act_grad(0, (2, 1, 0), False, inner)
    act_grad(1, (2, 1, 0), False, inner)
    act_grad(2, (2, 1), False, inner)
    reduce_middle(0)
    frame_send(0, half, half, 0)
    frame_send(1, 0, 1, 1)
    frame_send(1, NR - 1, 1, 1)
    frame_send(1, 1, NR - 2, 2)
    halo[0].wait_recv()
    halo[1].wait_recv()
    clear_rows(range(NF))
    act_grad(0, (2, 1, 0), False, outer)
    act_grad(1, (2, 1, 0), False, outer)
    act_grad(2, (2, 1), False, outer)
    act_grad(3, (2,), False)
    sums = group_sum(reduce_end(0))
    mean = sums[0:1] / MEMBERS
    variance = sums[1:2] / MEMBERS - mean * mean
    inv = lax.rsqrt(variance + 1e-06)
    copy_gain.wait()
    copy_shift.wait()
    gain, shift = gain_v[...], shift_v[...]

    pixel = lax.broadcasted_iota(jnp.int32, (C, W), 1)

    def activate(t):
        for r in range(NR):
            normed = (act_v[t, r].astype(F32) - mean) * inv
            scaled = normed * gain + shift
            sigma = jax.nn.sigmoid(scaled)
            dv_v[t, r] = sigma * (1.0 + scaled * (1.0 - sigma))
            turned = (scaled * sigma).T
            at_v[t, r, 0:C] = jnp.where(pixel > 0, pltpu.roll(turned, 1, 1), 0.0).astype(BF16)
            at_v[t, r, C : 2 * C] = turned.astype(BF16)
            at_v[t, r, 2 * C : 3 * C] = jnp.where(pixel < W - 1, pltpu.roll(turned, W - 1, 1), 0.0).astype(BF16)

    def weight_part(a, t):
        lhs = jnp.concatenate([at_v[t, r] for r in range(NR)], axis=1)
        rhs = jnp.concatenate(
            [grad_v[t + 2 - a, 2 - b : 2 - b + NR].reshape(ROWS, C) for b in range(3)], axis=1
        )
        o = jnp.dot(lhs, rhs, preferred_element_type=F32)
        for b in range(3):
            v = o[:, b * C : (b + 1) * C].reshape(3, C, C)
            at = pl.ds((2 - a) * 3, 3)
            wacc[b, at] = v + wacc[b, at] if t else v

    half0 = core * 64
    twin = chip(z, y, x, 1 - core)
    place = (x, y, z)
    groups = ((0, 3), (3, 6), (6, 9))

    def on_axis(b, k, cc=core):
        return (chip(z, y, k, cc), chip(z, k, x, cc), chip(k, y, x, cc))[b]

    def span_of(start, size):
        return pl.ds(pl.multiple_of(start, 16), size)

    def core_send(g):
        at = pl.ds(3 * g, 3)
        src = wacc.at[:, at, span_of(64 - half0, 64)]
        remote(src, rs_core.at[:, at], send_sem.at[0], c_r.at[g], twin).start()

    def axis_send(g):
        at = pl.ds(3 * g, 3)
        take(rs_core.at[:, at], c_r.at[g])
        here = span_of(half0, 64)
        for b in range(3):
            wacc[b, at, here] = wacc[b, at, here] + rs_core[b, at]
            for d in range(1, 4):
                k = (place[b] + d) % 4
                src = wacc.at[b, at, span_of(half0 + k * 16, 16)]
                to = rs_axis.at[0, b, place[b], at]
                remote(src, to, send_sem.at[0], x_r.at[g, b], on_axis(b, k)).start()

    def mine(b):
        return span_of(half0 + place[b] * 16, 16)

    def exchange(k, g, b, value, recv):
        lo, hi = groups[g]
        axis = (b + k) % 3
        slot = rs_axis.at[k, b, place[axis], pl.ds(lo, hi - lo)]
        slot[...] = value
        for d in range(1, 4):
            remote(slot, slot, send_sem.at[0], recv.at[g, b], on_axis(axis, (place[axis] + d) % 4)).start()

    def along_second(g, b):
        lo, hi = groups[g]
        take(rs_axis.at[0, b, pl.ds(0, 3), pl.ds(lo, 3)], x_r.at[g, b])
        rs_axis[0, b, place[b], pl.ds(lo, hi - lo)] = wacc[b, lo:hi, mine(b)]
        exchange(1, g, b, rs_axis[0, b, :, lo:hi].sum(axis=0), y_r)

    def along_third(g, b):
        lo, hi = groups[g]
        take(rs_axis.at[1, b, pl.ds(0, 3), pl.ds(lo, hi - lo)], y_r.at[g, b])
        exchange(2, g, b, rs_axis[1, b, :, lo:hi].sum(axis=0), z_r)

    def gather_axis(g, b):
        lo, hi = groups[g]
        take(rs_axis.at[2, b, pl.ds(0, 3), pl.ds(lo, hi - lo)], z_r.at[g, b])
        total = rs_axis[2, b, :, lo:hi].sum(axis=0) * SCALE
        wout[b, lo:hi, mine(b)] = total.astype(BF16)
        tiles = wout.at[b, pl.ds(lo, hi - lo), mine(b)]
        for d in range(1, 8) if g == 2 else (2, 4, 6):
            to = on_axis(b, (place[b] + d // 2) % 4, (core + d) % 2)
            remote(tiles, tiles, send_sem.at[0], gx_r.at[g, b], to).start()

    def gather_core(g, b):
        lo, hi = groups[g]
        take(wout.at[b, pl.ds(lo, hi - lo), pl.ds(0, 48)], gx_r.at[g, b])
        part = wout.at[b, pl.ds(lo, hi - lo), span_of(half0, 64)]
        remote(part, part, send_sem.at[0], gc_r.at[g, b], twin).start()

    def complete(g, b):
        lo, hi = groups[g]
        if g == 2:
            take(wout.at[b, pl.ds(lo, hi - lo), pl.ds(0, 112)], gx_r.at[g, b])
        else:
            take(wout.at[b, pl.ds(lo, hi - lo), pl.ds(0, 64)], gc_r.at[g, b])
        wide[2 - g, b] = wout[b, lo:hi].astype(F32)

    def each(stage, g):
        for b in range(3):
            stage(g, b)

    def clear_frame(f):
        @pl.when(span == 7)
        def _():
            def clear(i, _):
                grad_v[f, i] = jnp.zeros((W, C), BF16)
                return 0

            lax.fori_loop(0, NR + 2, clear, 0)

    def outer_rows(n, f):
        halo[n].wait_recv()
        halo[n].wait_send()
        halo[n + 1].wait_recv()
        halo[n + 1].wait_send()
        clear_rows((f,))
        clear_frame(f)

    activate(0)
    weight_part(2, 0)
    activate(1)
    weight_part(2, 1)
    activate(2)
    arrive(0)
    halo[2].start()
    halo[3].start()
    weight_part(2, 2)
    activate(3)
    arrive(1)
    halo[4].start()
    halo[5].start()
    weight_part(2, 3)
    core_send(0)
    for t in range(3):
        weight_part(1, t)
    for t in range(2):
        weight_part(0, t)
    axis_send(0)
    outer_rows(2, NF)
    weight_part(1, 3)
    core_send(1)
    weight_part(0, 2)
    arrive(2)
    outer_rows(4, NF + 1)
    weight_part(0, 3)
    core_send(2)
    axis_send(1)
    act_grad(3, (1, 0), True, first)
    axis_send(2)
    each(along_second, 0)
    act_grad(3, (1, 0), True, second)
    act_grad(2, (0,), True)

    def finish(i, carry):
        t, r = i // NR, i % NR
        normed = (act_v[t, r].astype(F32) - mean) * inv
        pre = ag_v[t, r] * dv_v[t, r]
        ag_v[t, r] = pre
        return carry[0] + fold(pre * normed), carry[1] + fold(pre)

    gain_sum, shift_sum = lax.fori_loop(0, NF * NR, finish, (zero8, zero8), unroll=2)
    reduce_start(1, stacked(gain_sum, shift_sum, bias))
    each(along_second, 1)
    each(along_second, 2)
    each(along_third, 0)
    each(along_third, 1)
    reduce_middle(1)
    each(along_third, 2)
    each(gather_axis, 0)
    each(gather_axis, 1)
    each(gather_axis, 2)
    total = reduce_end(1)
    scaled_sums = total * SCALE
    gain_out[...] = scaled_sums[0:1]
    shift_out[...] = scaled_sums[1:2]
    bias_out[...] = scaled_sums[2:3]
    means = group_sum(total * gain) / MEMBERS
    mean_two, mean_one = means[0:1], means[1:2]

    def result(i, _):
        t, r = i // NR, i % NR
        normed = (act_v[t, r].astype(F32) - mean) * inv
        outb[t, r] = (inv * (gain * ag_v[t, r] - mean_one - normed * mean_two)).astype(BF16)
        return 0

    lax.fori_loop(0, NF * NR, result, 0, unroll=2)
    each(gather_core, 0)
    each(gather_core, 1)
    for g in range(GROUPS):
        each(complete, g)
    sent(all_sent, send_sem.at[0])


def write_out(in_ref, w_ref, gain_ref, shift_ref, bias_ref, out_hbm, wout_hbm, gain_hbm, shift_hbm, bias_hbm, sem):
    pairs = [(w_ref.at[a], wout_hbm.at[a]) for a in range(3)]
    pairs += [(in_ref, out_hbm), (gain_ref, gain_hbm), (shift_ref, shift_hbm), (bias_ref, bias_hbm)]
    copies = [pltpu.make_async_copy(src, to, sem.at[n]) for n, (src, to) in enumerate(pairs)]
    for copy in copies:
        copy.start()
    for copy in copies:
        copy.wait()


def body(activations, cotangent, conv_weight, norm_gain, norm_shift):
    anywhere = pl.BlockSpec(memory_space=pl.ANY)
    vmem = pl.BlockSpec(memory_space=pltpu.VMEM)
    dma = pltpu.SemaphoreType.DMA
    results = pl.pallas_call(
        kernel,
        out_shape=(
            pltpu.VMEM((NF, NR, W, C), BF16),
            pltpu.VMEM((3, 3, 3, C, C), F32),
            pltpu.VMEM((1, C), F32),
            pltpu.VMEM((1, C), F32),
            pltpu.VMEM((1, C), F32),
        ),
        in_specs=[anywhere] * 5,
        out_specs=(vmem,) * 5,
        scratch_shapes=[
            pltpu.VMEM((1, C), F32),
            pltpu.VMEM((1, C), F32),
            pltpu.VMEM((NF, NR, W, C), BF16),
            pltpu.VMEM((NF + 2, NR + 2, W, C), BF16),
            pltpu.VMEM((9, 3 * C, C), BF16),
            pltpu.VMEM((NF, NR, 3 * C, W), BF16),
            pltpu.VMEM((NF, NR, W, C), F32),
            pltpu.VMEM((NF, NR, W, C), F32),
            pltpu.VMEM((3, 9, C, C), F32),
            pltpu.VMEM((3, 9, 64, C), F32),
            pltpu.VMEM((3, 3, 4, 9, 16, C), F32),
            pltpu.VMEM((3, 9, C, C), BF16),
            pltpu.VMEM((2, 2, 4, C), F32),
            pltpu.VMEM((2, 16, 4, C), F32),
            pltpu.VMEM((2, 8, 4, C), F32),
            pltpu.VMEM((SENT, C), F32),
            dma((NF + 4,)), dma((5,)), dma((6,)), dma((3,)), dma((2, 2)), dma((3,)), dma((3, 3)),
            dma((GROUPS, 3)), dma((GROUPS, 3)), dma((GROUPS, 3)), dma((2, 3)),
        ],
        compiler_params=pltpu.CompilerParams(
            collective_id=0, has_side_effects=True, vmem_limit_bytes=64_100_000
        ),
    )(
        activations,
        cotangent,
        conv_weight.reshape(9, 3 * C, C),
        norm_gain.reshape(1, C),
        norm_shift.reshape(1, C),
    )
    per_channel = jax.ShapeDtypeStruct((1, C), F32)
    input_grad, weight_grad, gain_grad, shift_grad, bias_grad = pl.pallas_call(
        write_out,
        out_shape=(
            jax.ShapeDtypeStruct((NF, NR, W, C), BF16),
            jax.ShapeDtypeStruct((3, 3, 3, C, C), F32),
            per_channel,
            per_channel,
            per_channel,
        ),
        in_specs=[vmem] * 5,
        out_specs=(anywhere,) * 5,
        scratch_shapes=[dma((7,))],
        compiler_params=pltpu.CompilerParams(vmem_limit_bytes=16 * 1024 * 1024),
    )(*results)
    return input_grad, weight_grad, gain_grad.reshape(C), shift_grad.reshape(C), bias_grad.reshape(C)


def solution(mesh):
    placed = (P("span", "slab", None, None), P("span", "slab", None, None), P(), P(), P())
    return jax.shard_map(
        body,
        mesh=mesh,
        in_specs=placed,
        out_specs=(P("span", "slab", None, None), P(), P(), P(), P()),
        check_vma=False,
    )
```

```python
import jax
import jax.numpy as jnp
from jax import lax
from jax.experimental import pallas as pl
from jax.experimental.pallas import tpu as pltpu
from jax.sharding import PartitionSpec as P

MESH = pl.DeviceIdType.MESH
F32 = jnp.float32
BF16 = jnp.bfloat16
NF, NR, W, C = 4, 8, 128, 128
ROWS = NR * W
CELLS = 32 * 128 * 128
MEMBERS = CELLS * 4
SCALE = float(CELLS) ** -0.5
SENT = 2 * NF * 64 + 2 * NR * 64 + 2 * (7 + 15) * 4 + 27 * 64 + 3 * 27 * 48 + 18 * 24 + 18 * 32 + 9 * 56
GROUPS = 3
FAR_FIRST = (2, 1, 3)
NT_DIMS = (((1,), (1,)), ((), ()))


def group_sum(v):
    lane = lax.broadcasted_iota(jnp.int32, v.shape, 1)
    v = v + jnp.where(lane % 2 == 0, pltpu.roll(v, C - 1, 1), pltpu.roll(v, 1, 1))
    return v + jnp.where(lane % 4 < 2, pltpu.roll(v, C - 2, 1), pltpu.roll(v, 2, 1))


def fold(v):
    return v.reshape(-1, 8, C).sum(axis=0)


def kernel(
    act_hbm, cot_hbm, w_hbm, gain_hbm, shift_hbm,
    outb, wide, gain_out, shift_out, bias_out,
    gain_v, shift_v, act_v, grad_v, w_v, at_v, ag_v, dv_v, wacc, rs_core, rs_axis, wout, stat, arb, ara,
    all_sent, loc_sem, send_sem, halo_r, frame_r, ar_r, c_r, x_r, y_r, z_r, gx_r, gc_r,
):
    span, slab = lax.axis_index("span"), lax.axis_index("slab")
    z, y = span // 2, (span % 2) * 2 + slab // 8
    xc = slab % 8
    x, core = xc // 2, xc % 2

    def chip(cz, cy, cx, cc=core):
        return (cz * 2 + cy // 2, (cy % 2) * 8 + cx * 2 + cc)

    barrier = pltpu.get_barrier_semaphore()
    above = (span, (slab + 15) % 16)
    below = (span, (slab + 1) % 16)
    greeted = [chip(z, y, (x + d // 2) % 4, (core + d) % 2) for d in range(1, 8)]
    greeted += [above, below]
    greeted += [chip((z + d // 4) % 4, (y + d % 4) % 4, x) for d in range(1, 16)]
    greeted += [chip(z, (y + d) % 4, x, 1 - core) for d in range(1, 4)]
    greeted += [chip((z + d) % 4, y, x, 1 - core) for d in range(1, 4)]

    def greet(devices):
        for device in devices:
            pl.semaphore_signal(barrier, inc=1, device_id=device, device_id_type=MESH)

    greet(greeted[:7])
    copies_act = [pltpu.make_async_copy(act_hbm.at[t], act_v.at[t], loc_sem.at[t]) for t in range(NF)]
    copy_cot = pltpu.make_async_copy(cot_hbm, grad_v.at[pl.ds(0, NF), pl.ds(1, NR)], loc_sem.at[NF])
    copy_w = pltpu.make_async_copy(w_hbm, w_v, loc_sem.at[NF + 1])
    copy_gain = pltpu.make_async_copy(gain_hbm, gain_v, loc_sem.at[NF + 2])
    copy_shift = pltpu.make_async_copy(shift_hbm, shift_v, loc_sem.at[NF + 3])
    for copy in copies_act:
        copy.start()
    greet(greeted[7:])

    def remote(src, dst, send, recv, device):
        return pltpu.make_async_remote_copy(
            src_ref=src, dst_ref=dst, send_sem=send, recv_sem=recv, device_id=device, device_id_type=MESH
        )

    def take(ref, recv):
        remote(ref, ref, recv, recv, below).wait_recv()

    def sent(ref, send):
        remote(ref, ref, send, send, below).wait_send()

    zero8 = jnp.zeros((8, C), F32)
    one, two = zero8, zero8
    for t in range(NF):
        copies_act[t].wait()
        if t == NF - 2:
            copy_cot.start()
        if t == NF - 1:
            for copy in (copy_w, copy_gain, copy_shift):
                copy.start()

        def local_sums(r, carry, t=t):
            v = act_v[t, r].astype(F32)
            return carry[0] + fold(v), carry[1] + fold(v * v)

        one, two = lax.fori_loop(0, NR, local_sums, (one, two), unroll=2)
    row = lax.broadcasted_iota(jnp.int32, (4, C), 0)

    def stacked(*sums):
        value = jnp.zeros((4, C), F32)
        for n, v in enumerate(sums):
            value = jnp.where(row == n, jnp.broadcast_to(v.sum(axis=0, keepdims=True), (4, C)), value)
        return value

    def in_yz(q):
        return chip(q // 4, q % 4, x)

    def in_row(j):
        return chip(z, y, j // 2, j % 2)

    yz = z * 4 + y

    def reduce_start(n, value):
        stat[n, 0] = value
        ara[n, xc] = value
        for d in (4, 5, 2, 3, 6, 7, 1):
            remote(stat.at[n, 0], ara.at[n, xc], send_sem.at[0], ar_r.at[n, 0], in_row((x + d // 2) % 4 * 2 + (core + d) % 2)).start()

    def reduce_middle(n):
        take(ara.at[n, pl.ds(0, 7)], ar_r.at[n, 0])
        value = ara[n].sum(axis=0)
        stat[n, 1] = value
        arb[n, yz] = value
        for d in (10, 6, 14, 9, 11, 5, 7, 13, 15, 8, 2, 4, 12, 1, 3):
            to = (z + d // 4) % 4 * 4 + (y + d % 4) % 4
            remote(stat.at[n, 1], arb.at[n, yz], send_sem.at[0], ar_r.at[n, 1], in_yz(to)).start()

    def reduce_end(n):
        take(arb.at[n, pl.ds(0, 15)], ar_r.at[n, 1])
        return arb[n].sum(axis=0)

    pl.semaphore_wait(barrier, len(greeted))

    halo = [
        remote(cot_hbm.at[:, 0], grad_v.at[pl.ds(0, NF), NR + 1], send_sem.at[0], halo_r.at[0], above),
        remote(cot_hbm.at[:, NR - 1], grad_v.at[pl.ds(0, NF), 0], send_sem.at[0], halo_r.at[1], below),
        remote(grad_v.at[NF, 1], grad_v.at[NF, NR + 1], send_sem.at[1], halo_r.at[2], above),
        remote(grad_v.at[NF, NR], grad_v.at[NF, 0], send_sem.at[2], halo_r.at[3], below),
        remote(grad_v.at[NF + 1, 1], grad_v.at[NF + 1, NR + 1], send_sem.at[3], halo_r.at[4], above),
        remote(grad_v.at[NF + 1, NR], grad_v.at[NF + 1, 0], send_sem.at[4], halo_r.at[5], below),
    ]
    before = ((span + 7) % 8, slab)

    def frame_send(f, start, size, n):
        to = grad_v.at[NF + f, pl.ds(1 + start, size)]
        remote(cot_hbm.at[f, pl.ds(start, size)], to, send_sem.at[0], frame_r.at[n], before).start()

    def arrive(n):
        take(grad_v.at[NF, pl.ds(0, (NR, 2, NR - 2)[n])], frame_r.at[n])

    reduce_start(0, stacked(one, two))
    halo[0].start()
    halo[1].start()
    frame_send(0, 0, 5, 0)

    copy_cot.wait()

    def bias_local(i, carry):
        return carry + fold(grad_v[i // NR, 1 + i % NR].astype(F32))

    bias = lax.fori_loop(0, NF * NR, bias_local, zero8, unroll=2)

    def clear_rows(frames):
        @pl.when(slab == 0)
        def _():
            for f in frames:
                grad_v[f, 0] = jnp.zeros((W, C), BF16)

        @pl.when(slab == 15)
        def _():
            for f in frames:
                grad_v[f, NR + 1] = jnp.zeros((W, C), BF16)

    def shifted_sum(o):
        o = o.reshape(-1, W, 3 * C)
        pixel = lax.broadcasted_iota(jnp.int32, (1, W, C), 1)
        left = pltpu.roll(o[:, :, :C], W - 1, 1)
        right = pltpu.roll(o[:, :, 2 * C :], 1, 1)
        return o[:, :, C : 2 * C] + jnp.where(pixel < W - 1, left, 0.0) + jnp.where(pixel > 0, right, 0.0)

    def act_grad(t, taps, add, parts=((0, 4), (4, 4))):
        rhs = jnp.concatenate([w_v[a * 3 + b] for a in taps for b in range(3)], axis=1)
        for r, n in parts:
            lhs = jnp.concatenate(
                [
                    grad_v[t + 2 - a, r + 2 - b : r + 2 - b + n].reshape(n * W, C)
                    for a in taps
                    for b in range(3)
                ],
                axis=1,
            )
            o = shifted_sum(lax.dot_general(lhs, rhs, NT_DIMS, preferred_element_type=F32))
            if add:
                o = o + ag_v[t, r : r + n]
            ag_v[t, r : r + n] = o

    inner, outer = ((2, 4),), ((0, 2), (6, 2))
    first, second = ((0, 4),), ((4, 4),)
    copy_w.wait()
    act_grad(0, (2, 1, 0), False, inner)
    act_grad(1, (2, 1, 0), False, inner)
    act_grad(2, (2, 1), False, inner)
    reduce_middle(0)
    frame_send(0, 5, NR - 5, 0)
    frame_send(1, 0, 1, 1)
    frame_send(1, NR - 1, 1, 1)
    frame_send(1, 1, NR - 2, 2)
    halo[0].wait_recv()
    halo[1].wait_recv()
    clear_rows(range(NF))
    act_grad(0, (2, 1, 0), False, outer)
    act_grad(1, (2, 1, 0), False, outer)
    act_grad(2, (2, 1), False, outer)
    act_grad(3, (2,), False)
    sums = group_sum(reduce_end(0))
    mean = sums[0:1] / MEMBERS
    variance = sums[1:2] / MEMBERS - mean * mean
    inv = lax.rsqrt(variance + 1e-06)
    copy_gain.wait()
    copy_shift.wait()
    gain, shift = gain_v[...], shift_v[...]

    pixel = lax.broadcasted_iota(jnp.int32, (C, W), 1)

    def activate(t):
        for r in range(NR):
            normed = (act_v[t, r].astype(F32) - mean) * inv
            scaled = normed * gain + shift
            sigma = jax.nn.sigmoid(scaled)
            dv_v[t, r] = sigma * (1.0 + scaled * (1.0 - sigma))
            turned = (scaled * sigma).T
            at_v[t, r, 0:C] = jnp.where(pixel > 0, pltpu.roll(turned, 1, 1), 0.0).astype(BF16)
            at_v[t, r, C : 2 * C] = turned.astype(BF16)
            at_v[t, r, 2 * C : 3 * C] = jnp.where(pixel < W - 1, pltpu.roll(turned, W - 1, 1), 0.0).astype(BF16)

    def weight_part(a, t):
        lhs = jnp.concatenate([at_v[t, r] for r in range(NR)], axis=1)
        rhs = jnp.concatenate(
            [grad_v[t + 2 - a, 2 - b : 2 - b + NR].reshape(ROWS, C) for b in range(3)], axis=1
        )
        o = jnp.dot(lhs, rhs, preferred_element_type=F32)
        for b in range(3):
            v = o[:, b * C : (b + 1) * C].reshape(3, C, C)
            at = pl.ds((2 - a) * 3, 3)
            wacc[b, at] = v + wacc[b, at] if t else v

    half0 = core * 64
    twin = chip(z, y, x, 1 - core)
    place = (x, y, z)
    groups = ((0, 3), (3, 6), (6, 9))

    def on_axis(b, k, cc=core):
        return (chip(z, y, k, cc), chip(z, k, x, cc), chip(k, y, x, cc))[b]

    def span_of(start, size):
        return pl.ds(pl.multiple_of(start, 16), size)

    def core_send(g):
        at = pl.ds(3 * g, 3)
        src = wacc.at[:, at, span_of(64 - half0, 64)]
        remote(src, rs_core.at[:, at], send_sem.at[0], c_r.at[g], twin).start()

    def axis_send(g):
        at = pl.ds(3 * g, 3)
        take(rs_core.at[:, at], c_r.at[g])
        here = span_of(half0, 64)
        for b in range(3):
            wacc[b, at, here] = wacc[b, at, here] + rs_core[b, at]
            for d in FAR_FIRST:
                k = (place[b] + d) % 4
                src = wacc.at[b, at, span_of(half0 + k * 16, 16)]
                to = rs_axis.at[0, b, place[b], at]
                remote(src, to, send_sem.at[0], x_r.at[g, b], on_axis(b, k)).start()

    def mine(b):
        return span_of(half0 + place[b] * 16, 16)

    def exchange(k, g, b, value, recv):
        lo, hi = groups[g]
        axis = (b + k) % 3
        slot = rs_axis.at[k, b, place[axis], pl.ds(lo, hi - lo)]
        slot[...] = value
        for d in FAR_FIRST:
            remote(slot, slot, send_sem.at[0], recv.at[g, b], on_axis(axis, (place[axis] + d) % 4)).start()

    def along_second(g, b):
        lo, hi = groups[g]
        take(rs_axis.at[0, b, pl.ds(0, 3), pl.ds(lo, 3)], x_r.at[g, b])
        rs_axis[0, b, place[b], pl.ds(lo, hi - lo)] = wacc[b, lo:hi, mine(b)]
        exchange(1, g, b, rs_axis[0, b, :, lo:hi].sum(axis=0), y_r)

    def along_third(g, b):
        lo, hi = groups[g]
        take(rs_axis.at[1, b, pl.ds(0, 3), pl.ds(lo, hi - lo)], y_r.at[g, b])
        exchange(2, g, b, rs_axis[1, b, :, lo:hi].sum(axis=0), z_r)

    def gather_axis(g, b):
        lo, hi = groups[g]
        take(rs_axis.at[2, b, pl.ds(0, 3), pl.ds(lo, hi - lo)], z_r.at[g, b])
        total = rs_axis[2, b, :, lo:hi].sum(axis=0) * SCALE
        wout[b, lo:hi, mine(b)] = total.astype(BF16)
        tiles = wout.at[b, pl.ds(lo, hi - lo), mine(b)]
        for d in (4, 5, 2, 3, 6, 7, 1) if g == 2 else (4, 2, 6):
            to = on_axis(b, (place[b] + d // 2) % 4, (core + d) % 2)
            remote(tiles, tiles, send_sem.at[0], gx_r.at[g, b], to).start()

    def gather_core(g, b):
        lo, hi = groups[g]
        take(wout.at[b, pl.ds(lo, hi - lo), pl.ds(0, 48)], gx_r.at[g, b])
        part = wout.at[b, pl.ds(lo, hi - lo), span_of(half0, 64)]
        remote(part, part, send_sem.at[0], gc_r.at[g, b], twin).start()

    def complete(g, b):
        lo, hi = groups[g]
        if g == 2:
            take(wout.at[b, pl.ds(lo, hi - lo), pl.ds(0, 112)], gx_r.at[g, b])
        else:
            take(wout.at[b, pl.ds(lo, hi - lo), pl.ds(0, 64)], gc_r.at[g, b])
        wide[2 - g, b] = wout[b, lo:hi].astype(F32)

    def each(stage, g):
        for b in range(3):
            stage(g, b)

    def clear_frame(f):
        @pl.when(span == 7)
        def _():
            def clear(i, _):
                grad_v[f, i] = jnp.zeros((W, C), BF16)
                return 0

            lax.fori_loop(0, NR + 2, clear, 0)

    def outer_rows(n, f):
        halo[n].wait_recv()
        halo[n].wait_send()
        halo[n + 1].wait_recv()
        halo[n + 1].wait_send()
        clear_rows((f,))
        clear_frame(f)

    activate(0)
    weight_part(2, 0)
    activate(1)
    weight_part(2, 1)
    activate(2)
    arrive(0)
    halo[2].start()
    halo[3].start()
    weight_part(2, 2)
    activate(3)
    arrive(1)
    halo[4].start()
    halo[5].start()
    weight_part(2, 3)
    core_send(0)
    for t in range(3):
        weight_part(1, t)
    for t in range(2):
        weight_part(0, t)
    axis_send(0)
    outer_rows(2, NF)
    weight_part(1, 3)
    core_send(1)
    weight_part(0, 2)
    arrive(2)
    outer_rows(4, NF + 1)
    weight_part(0, 3)
    core_send(2)
    axis_send(1)
    act_grad(3, (1, 0), True, first)
    axis_send(2)
    each(along_second, 0)
    act_grad(3, (1, 0), True, second)
    act_grad(2, (0,), True)

    def finish(i, carry):
        t, r = i // NR, i % NR
        normed = (act_v[t, r].astype(F32) - mean) * inv
        pre = ag_v[t, r] * dv_v[t, r]
        ag_v[t, r] = pre
        return carry[0] + fold(pre * normed), carry[1] + fold(pre)

    gain_sum, shift_sum = lax.fori_loop(0, NF * NR, finish, (zero8, zero8), unroll=2)
    reduce_start(1, stacked(gain_sum, shift_sum, bias))
    each(along_second, 1)
    each(along_second, 2)
    each(along_third, 0)
    each(along_third, 1)
    reduce_middle(1)
    each(along_third, 2)
    each(gather_axis, 0)
    each(gather_axis, 1)
    each(gather_axis, 2)
    total = reduce_end(1)
    scaled_sums = total * SCALE
    gain_out[...] = scaled_sums[0:1]
    shift_out[...] = scaled_sums[1:2]
    bias_out[...] = scaled_sums[2:3]
    means = group_sum(total * gain) / MEMBERS
    mean_two, mean_one = means[0:1], means[1:2]

    def result(i, _):
        t, r = i // NR, i % NR
        normed = (act_v[t, r].astype(F32) - mean) * inv
        outb[t, r] = (inv * (gain * ag_v[t, r] - mean_one - normed * mean_two)).astype(BF16)
        return 0

    lax.fori_loop(0, NF * NR, result, 0, unroll=2)
    each(gather_core, 0)
    each(gather_core, 1)
    for g in range(GROUPS):
        each(complete, g)
    sent(all_sent, send_sem.at[0])


def write_out(in_ref, w_ref, gain_ref, shift_ref, bias_ref, out_hbm, wout_hbm, gain_hbm, shift_hbm, bias_hbm, sem):
    pairs = [(w_ref.at[a], wout_hbm.at[a]) for a in range(3)]
    pairs += [(in_ref, out_hbm), (gain_ref, gain_hbm), (shift_ref, shift_hbm), (bias_ref, bias_hbm)]
    copies = [pltpu.make_async_copy(src, to, sem.at[n]) for n, (src, to) in enumerate(pairs)]
    for copy in copies:
        copy.start()
    for copy in copies:
        copy.wait()


def body(activations, cotangent, conv_weight, norm_gain, norm_shift):
    anywhere = pl.BlockSpec(memory_space=pl.ANY)
    vmem = pl.BlockSpec(memory_space=pltpu.VMEM)
    dma = pltpu.SemaphoreType.DMA
    results = pl.pallas_call(
        kernel,
        out_shape=(
            pltpu.VMEM((NF, NR, W, C), BF16),
            pltpu.VMEM((3, 3, 3, C, C), F32),
            pltpu.VMEM((1, C), F32),
            pltpu.VMEM((1, C), F32),
            pltpu.VMEM((1, C), F32),
        ),
        in_specs=[anywhere] * 5,
        out_specs=(vmem,) * 5,
        scratch_shapes=[
            pltpu.VMEM((1, C), F32),
            pltpu.VMEM((1, C), F32),
            pltpu.VMEM((NF, NR, W, C), BF16),
            pltpu.VMEM((NF + 2, NR + 2, W, C), BF16),
            pltpu.VMEM((9, 3 * C, C), BF16),
            pltpu.VMEM((NF, NR, 3 * C, W), BF16),
            pltpu.VMEM((NF, NR, W, C), F32),
            pltpu.VMEM((NF, NR, W, C), F32),
            pltpu.VMEM((3, 9, C, C), F32),
            pltpu.VMEM((3, 9, 64, C), F32),
            pltpu.VMEM((3, 3, 4, 9, 16, C), F32),
            pltpu.VMEM((3, 9, C, C), BF16),
            pltpu.VMEM((2, 2, 4, C), F32),
            pltpu.VMEM((2, 16, 4, C), F32),
            pltpu.VMEM((2, 8, 4, C), F32),
            pltpu.VMEM((SENT, C), F32),
            dma((NF + 4,)), dma((5,)), dma((6,)), dma((3,)), dma((2, 2)), dma((3,)), dma((3, 3)),
            dma((GROUPS, 3)), dma((GROUPS, 3)), dma((GROUPS, 3)), dma((2, 3)),
        ],
        compiler_params=pltpu.CompilerParams(
            collective_id=0, has_side_effects=True, vmem_limit_bytes=64_100_000
        ),
    )(
        activations,
        cotangent,
        conv_weight.reshape(9, 3 * C, C),
        norm_gain.reshape(1, C),
        norm_shift.reshape(1, C),
    )
    per_channel = jax.ShapeDtypeStruct((1, C), F32)
    input_grad, weight_grad, gain_grad, shift_grad, bias_grad = pl.pallas_call(
        write_out,
        out_shape=(
            jax.ShapeDtypeStruct((NF, NR, W, C), BF16),
            jax.ShapeDtypeStruct((3, 3, 3, C, C), F32),
            per_channel,
            per_channel,
            per_channel,
        ),
        in_specs=[vmem] * 5,
        out_specs=(anywhere,) * 5,
        scratch_shapes=[dma((7,))],
        compiler_params=pltpu.CompilerParams(vmem_limit_bytes=16 * 1024 * 1024),
    )(*results)
    return input_grad, weight_grad, gain_grad.reshape(C), shift_grad.reshape(C), bias_grad.reshape(C)


def solution(mesh):
    placed = (P("span", "slab", None, None), P("span", "slab", None, None), P(), P(), P())
    return jax.shard_map(
        body,
        mesh=mesh,
        in_specs=placed,
        out_specs=(P("span", "slab", None, None), P(), P(), P(), P()),
        check_vma=False,
    )
```

```python
import jax
import jax.numpy as jnp
from jax import lax
from jax.experimental import pallas as pl
from jax.experimental.pallas import tpu as pltpu
from jax.sharding import PartitionSpec as P

MESH = pl.DeviceIdType.MESH
F32 = jnp.float32
BF16 = jnp.bfloat16
NF, NR, W, C = 4, 8, 128, 128
ROWS = NR * W
CELLS = 32 * 128 * 128
MEMBERS = CELLS * 4
SCALE = float(CELLS) ** -0.5
SENT = 2 * NF * 64 + 2 * NR * 64 + 2 * (7 + 15) * 4 + 27 * 64 + 3 * 27 * 48 + 18 * 24 + 18 * 32 + 9 * 56
GROUPS = 3
FAR_FIRST = (2, 1, 3)
NT_DIMS = (((1,), (1,)), ((), ()))


def group_sum(v):
    lane = lax.broadcasted_iota(jnp.int32, v.shape, 1)
    v = v + jnp.where(lane % 2 == 0, pltpu.roll(v, C - 1, 1), pltpu.roll(v, 1, 1))
    return v + jnp.where(lane % 4 < 2, pltpu.roll(v, C - 2, 1), pltpu.roll(v, 2, 1))


def fold(v):
    return v.reshape(-1, 8, C).sum(axis=0)


def kernel(
    act_hbm, cot_hbm, w_hbm, gain_hbm, shift_hbm,
    outb, wide, gain_out, shift_out, bias_out,
    gain_v, shift_v, act_v, grad_v, w_v, at_v, ag_v, dv_v, wacc, rs_core, rs_axis, wout, stat, arb, ara,
    all_sent, loc_sem, send_sem, halo_r, frame_r, ar_r, c_r, x_r, y_r, z_r, gx_r, gc_r,
):
    span, slab = lax.axis_index("span"), lax.axis_index("slab")
    z, y = span // 2, (span % 2) * 2 + slab // 8
    xc = slab % 8
    x, core = xc // 2, xc % 2

    def chip(cz, cy, cx, cc=core):
        return (cz * 2 + cy // 2, (cy % 2) * 8 + cx * 2 + cc)

    barrier = pltpu.get_barrier_semaphore()
    above = (span, (slab + 15) % 16)
    below = (span, (slab + 1) % 16)
    greeted = [chip(z, y, (x + d // 2) % 4, (core + d) % 2) for d in range(1, 8)]
    greeted += [above, below]
    greeted += [chip((z + d // 4) % 4, (y + d % 4) % 4, x) for d in range(1, 16)]
    greeted += [chip(z, (y + d) % 4, x, 1 - core) for d in range(1, 4)]
    greeted += [chip((z + d) % 4, y, x, 1 - core) for d in range(1, 4)]

    def greet(devices):
        for device in devices:
            pl.semaphore_signal(barrier, inc=1, device_id=device, device_id_type=MESH)

    greet(greeted[:7])
    copies_act = [pltpu.make_async_copy(act_hbm.at[t], act_v.at[t], loc_sem.at[t]) for t in range(NF)]
    copy_cot = pltpu.make_async_copy(cot_hbm, grad_v.at[pl.ds(0, NF), pl.ds(1, NR)], loc_sem.at[NF])
    copy_w = pltpu.make_async_copy(w_hbm, w_v, loc_sem.at[NF + 1])
    copy_gain = pltpu.make_async_copy(gain_hbm, gain_v, loc_sem.at[NF + 2])
    copy_shift = pltpu.make_async_copy(shift_hbm, shift_v, loc_sem.at[NF + 3])
    for copy in copies_act:
        copy.start()
    greet(greeted[7:])

    def remote(src, dst, send, recv, device):
        return pltpu.make_async_remote_copy(
            src_ref=src, dst_ref=dst, send_sem=send, recv_sem=recv, device_id=device, device_id_type=MESH
        )

    def take(ref, recv):
        remote(ref, ref, recv, recv, below).wait_recv()

    def sent(ref, send):
        remote(ref, ref, send, send, below).wait_send()

    zero8 = jnp.zeros((8, C), F32)
    one, two = zero8, zero8
    for t in range(NF):
        copies_act[t].wait()
        if t == NF - 2:
            copy_cot.start()
        if t == NF - 1:
            for copy in (copy_w, copy_gain, copy_shift):
                copy.start()

        def local_sums(r, carry, t=t):
            v = act_v[t, r].astype(F32)
            return carry[0] + fold(v), carry[1] + fold(v * v)

        one, two = lax.fori_loop(0, NR, local_sums, (one, two), unroll=2)
    row = lax.broadcasted_iota(jnp.int32, (4, C), 0)

    def stacked(*sums):
        value = jnp.zeros((4, C), F32)
        for n, v in enumerate(sums):
            value = jnp.where(row == n, jnp.broadcast_to(v.sum(axis=0, keepdims=True), (4, C)), value)
        return value

    def in_yz(q):
        return chip(q // 4, q % 4, x)

    def in_row(j):
        return chip(z, y, j // 2, j % 2)

    yz = z * 4 + y

    def reduce_start(n, value):
        stat[n, 0] = value
        ara[n, xc] = value
        for d in (4, 5, 2, 3, 6, 7, 1):
            remote(stat.at[n, 0], ara.at[n, xc], send_sem.at[0], ar_r.at[n, 0], in_row((x + d // 2) % 4 * 2 + (core + d) % 2)).start()

    def reduce_middle(n):
        take(ara.at[n, pl.ds(0, 7)], ar_r.at[n, 0])
        value = ara[n].sum(axis=0)
        stat[n, 1] = value
        arb[n, yz] = value
        for d in (10, 6, 14, 9, 11, 5, 7, 13, 15, 8, 2, 4, 12, 1, 3):
            to = (z + d // 4) % 4 * 4 + (y + d % 4) % 4
            remote(stat.at[n, 1], arb.at[n, yz], send_sem.at[0], ar_r.at[n, 1], in_yz(to)).start()

    def reduce_end(n):
        take(arb.at[n, pl.ds(0, 15)], ar_r.at[n, 1])
        return arb[n].sum(axis=0)

    pl.semaphore_wait(barrier, len(greeted))

    halo = [
        remote(cot_hbm.at[:, 0], grad_v.at[pl.ds(0, NF), NR + 1], send_sem.at[0], halo_r.at[0], above),
        remote(cot_hbm.at[:, NR - 1], grad_v.at[pl.ds(0, NF), 0], send_sem.at[0], halo_r.at[1], below),
        remote(grad_v.at[NF, 1], grad_v.at[NF, NR + 1], send_sem.at[1], halo_r.at[2], above),
        remote(grad_v.at[NF, NR], grad_v.at[NF, 0], send_sem.at[2], halo_r.at[3], below),
        remote(grad_v.at[NF + 1, 1], grad_v.at[NF + 1, NR + 1], send_sem.at[3], halo_r.at[4], above),
        remote(grad_v.at[NF + 1, NR], grad_v.at[NF + 1, 0], send_sem.at[4], halo_r.at[5], below),
    ]
    before = ((span + 7) % 8, slab)

    def frame_send(f, start, size, n):
        to = grad_v.at[NF + f, pl.ds(1 + start, size)]
        remote(cot_hbm.at[f, pl.ds(start, size)], to, send_sem.at[0], frame_r.at[n], before).start()

    def arrive(n):
        take(grad_v.at[NF, pl.ds(0, (NR, 2, NR - 2)[n])], frame_r.at[n])

    reduce_start(0, stacked(one, two))
    frame_send(0, 0, 5, 0)
    halo[0].start()
    halo[1].start()

    copy_cot.wait()

    def bias_local(i, carry):
        return carry + fold(grad_v[i // NR, 1 + i % NR].astype(F32))

    bias = lax.fori_loop(0, NF * NR, bias_local, zero8, unroll=2)

    def clear_rows(frames):
        @pl.when(slab == 0)
        def _():
            for f in frames:
                grad_v[f, 0] = jnp.zeros((W, C), BF16)

        @pl.when(slab == 15)
        def _():
            for f in frames:
                grad_v[f, NR + 1] = jnp.zeros((W, C), BF16)

    def shifted_sum(o):
        o = o.reshape(-1, W, 3 * C)
        pixel = lax.broadcasted_iota(jnp.int32, (1, W, C), 1)
        left = pltpu.roll(o[:, :, :C], W - 1, 1)
        right = pltpu.roll(o[:, :, 2 * C :], 1, 1)
        return o[:, :, C : 2 * C] + jnp.where(pixel < W - 1, left, 0.0) + jnp.where(pixel > 0, right, 0.0)

    def act_grad(t, taps, add, parts=((0, 4), (4, 4))):
        rhs = jnp.concatenate([w_v[a * 3 + b] for a in taps for b in range(3)], axis=1)
        for r, n in parts:
            lhs = jnp.concatenate(
                [
                    grad_v[t + 2 - a, r + 2 - b : r + 2 - b + n].reshape(n * W, C)
                    for a in taps
                    for b in range(3)
                ],
                axis=1,
            )
            o = shifted_sum(lax.dot_general(lhs, rhs, NT_DIMS, preferred_element_type=F32))
            if add:
                o = o + ag_v[t, r : r + n]
            ag_v[t, r : r + n] = o

    inner, outer = ((2, 4),), ((0, 2), (6, 2))
    first, second = ((0, 4),), ((4, 4),)
    copy_w.wait()
    act_grad(0, (2, 1, 0), False, inner)
    act_grad(1, (2, 1, 0), False, inner)
    act_grad(2, (2, 1), False, inner)
    reduce_middle(0)
    frame_send(0, 5, NR - 5, 0)
    frame_send(1, 0, 1, 1)
    frame_send(1, NR - 1, 1, 1)
    frame_send(1, 1, NR - 2, 2)
    halo[0].wait_recv()
    halo[1].wait_recv()
    clear_rows(range(NF))
    act_grad(0, (2, 1, 0), False, outer)
    act_grad(1, (2, 1, 0), False, outer)
    act_grad(2, (2, 1), False, outer)
    act_grad(3, (2,), False)
    sums = group_sum(reduce_end(0))
    mean = sums[0:1] / MEMBERS
    variance = sums[1:2] / MEMBERS - mean * mean
    inv = lax.rsqrt(variance + 1e-06)
    copy_gain.wait()
    copy_shift.wait()
    gain, shift = gain_v[...], shift_v[...]

    pixel = lax.broadcasted_iota(jnp.int32, (C, W), 1)

    def activate(t):
        for r in range(NR):
            normed = (act_v[t, r].astype(F32) - mean) * inv
            scaled = normed * gain + shift
            sigma = jax.nn.sigmoid(scaled)
            dv_v[t, r] = sigma * (1.0 + scaled * (1.0 - sigma))
            turned = (scaled * sigma).T
            at_v[t, r, 0:C] = jnp.where(pixel > 0, pltpu.roll(turned, 1, 1), 0.0).astype(BF16)
            at_v[t, r, C : 2 * C] = turned.astype(BF16)
            at_v[t, r, 2 * C : 3 * C] = jnp.where(pixel < W - 1, pltpu.roll(turned, W - 1, 1), 0.0).astype(BF16)

    def weight_part(a, t):
        lhs = jnp.concatenate([at_v[t, r] for r in range(NR)], axis=1)
        rhs = jnp.concatenate(
            [grad_v[t + 2 - a, 2 - b : 2 - b + NR].reshape(ROWS, C) for b in range(3)], axis=1
        )
        o = jnp.dot(lhs, rhs, preferred_element_type=F32)
        for b in range(3):
            v = o[:, b * C : (b + 1) * C].reshape(3, C, C)
            at = pl.ds((2 - a) * 3, 3)
            wacc[b, at] = v + wacc[b, at] if t else v

    half0 = core * 64
    twin = chip(z, y, x, 1 - core)
    place = (x, y, z)
    groups = ((0, 3), (3, 6), (6, 9))

    def on_axis(b, k, cc=core):
        return (chip(z, y, k, cc), chip(z, k, x, cc), chip(k, y, x, cc))[b]

    def span_of(start, size):
        return pl.ds(pl.multiple_of(start, 16), size)

    def core_send(g):
        at = pl.ds(3 * g, 3)
        src = wacc.at[:, at, span_of(64 - half0, 64)]
        remote(src, rs_core.at[:, at], send_sem.at[0], c_r.at[g], twin).start()

    def axis_send(g):
        at = pl.ds(3 * g, 3)
        take(rs_core.at[:, at], c_r.at[g])
        here = span_of(half0, 64)
        for b in range(3):
            wacc[b, at, here] = wacc[b, at, here] + rs_core[b, at]
            for d in FAR_FIRST:
                k = (place[b] + d) % 4
                src = wacc.at[b, at, span_of(half0 + k * 16, 16)]
                to = rs_axis.at[0, b, place[b], at]
                remote(src, to, send_sem.at[0], x_r.at[g, b], on_axis(b, k)).start()

    def mine(b):
        return span_of(half0 + place[b] * 16, 16)

    def exchange(k, g, b, value, recv):
        lo, hi = groups[g]
        axis = (b + k) % 3
        slot = rs_axis.at[k, b, place[axis], pl.ds(lo, hi - lo)]
        slot[...] = value
        for d in FAR_FIRST:
            remote(slot, slot, send_sem.at[0], recv.at[g, b], on_axis(axis, (place[axis] + d) % 4)).start()

    def along_second(g, b):
        lo, hi = groups[g]
        take(rs_axis.at[0, b, pl.ds(0, 3), pl.ds(lo, 3)], x_r.at[g, b])
        rs_axis[0, b, place[b], pl.ds(lo, hi - lo)] = wacc[b, lo:hi, mine(b)]
        exchange(1, g, b, rs_axis[0, b, :, lo:hi].sum(axis=0), y_r)

    def along_third(g, b):
        lo, hi = groups[g]
        take(rs_axis.at[1, b, pl.ds(0, 3), pl.ds(lo, hi - lo)], y_r.at[g, b])
        exchange(2, g, b, rs_axis[1, b, :, lo:hi].sum(axis=0), z_r)

    def gather_axis(g, b):
        lo, hi = groups[g]
        take(rs_axis.at[2, b, pl.ds(0, 3), pl.ds(lo, hi - lo)], z_r.at[g, b])
        total = rs_axis[2, b, :, lo:hi].sum(axis=0) * SCALE
        wout[b, lo:hi, mine(b)] = total.astype(BF16)
        tiles = wout.at[b, pl.ds(lo, hi - lo), mine(b)]
        for d in (4, 5, 2, 3, 6, 7, 1) if g == 2 else (4, 2, 6):
            to = on_axis(b, (place[b] + d // 2) % 4, (core + d) % 2)
            remote(tiles, tiles, send_sem.at[0], gx_r.at[g, b], to).start()

    def gather_core(g, b):
        lo, hi = groups[g]
        take(wout.at[b, pl.ds(lo, hi - lo), pl.ds(0, 48)], gx_r.at[g, b])
        part = wout.at[b, pl.ds(lo, hi - lo), span_of(half0, 64)]
        remote(part, part, send_sem.at[0], gc_r.at[g, b], twin).start()

    def complete(g, b):
        lo, hi = groups[g]
        if g == 2:
            take(wout.at[b, pl.ds(lo, hi - lo), pl.ds(0, 112)], gx_r.at[g, b])
        else:
            take(wout.at[b, pl.ds(lo, hi - lo), pl.ds(0, 64)], gc_r.at[g, b])
        wide[2 - g, b] = wout[b, lo:hi].astype(F32)

    def each(stage, g):
        for b in range(3):
            stage(g, b)

    def clear_frame(f):
        @pl.when(span == 7)
        def _():
            def clear(i, _):
                grad_v[f, i] = jnp.zeros((W, C), BF16)
                return 0

            lax.fori_loop(0, NR + 2, clear, 0)

    def outer_rows(n, f):
        halo[n].wait_recv()
        halo[n].wait_send()
        halo[n + 1].wait_recv()
        halo[n + 1].wait_send()
        clear_rows((f,))
        clear_frame(f)

    activate(0)
    weight_part(2, 0)
    activate(1)
    weight_part(2, 1)
    activate(2)
    arrive(0)
    halo[2].start()
    halo[3].start()
    weight_part(2, 2)
    activate(3)
    arrive(1)
    halo[4].start()
    halo[5].start()
    weight_part(2, 3)
    core_send(0)
    for t in range(3):
        weight_part(1, t)
    for t in range(2):
        weight_part(0, t)
    axis_send(0)
    outer_rows(2, NF)
    weight_part(1, 3)
    core_send(1)
    weight_part(0, 2)
    arrive(2)
    outer_rows(4, NF + 1)
    weight_part(0, 3)
    core_send(2)
    axis_send(1)
    act_grad(3, (1, 0), True, first)
    axis_send(2)
    each(along_second, 0)
    act_grad(3, (1, 0), True, second)
    act_grad(2, (0,), True)

    def finish(i, carry):
        t, r = i // NR, i % NR
        normed = (act_v[t, r].astype(F32) - mean) * inv
        pre = ag_v[t, r] * dv_v[t, r]
        ag_v[t, r] = pre
        return carry[0] + fold(pre * normed), carry[1] + fold(pre)

    gain_sum, shift_sum = lax.fori_loop(0, NF * NR, finish, (zero8, zero8), unroll=2)
    reduce_start(1, stacked(gain_sum, shift_sum, bias))
    each(along_second, 1)
    each(along_second, 2)
    each(along_third, 0)
    each(along_third, 1)
    reduce_middle(1)
    each(along_third, 2)
    each(gather_axis, 0)
    each(gather_axis, 1)
    each(gather_axis, 2)
    total = reduce_end(1)
    scaled_sums = total * SCALE
    gain_out[...] = scaled_sums[0:1]
    shift_out[...] = scaled_sums[1:2]
    bias_out[...] = scaled_sums[2:3]
    means = group_sum(total * gain) / MEMBERS
    mean_two, mean_one = means[0:1], means[1:2]

    def result(i, _):
        t, r = i // NR, i % NR
        normed = (act_v[t, r].astype(F32) - mean) * inv
        outb[t, r] = (inv * (gain * ag_v[t, r] - mean_one - normed * mean_two)).astype(BF16)
        return 0

    lax.fori_loop(0, NF * NR, result, 0, unroll=2)
    each(gather_core, 0)
    each(gather_core, 1)
    for g in range(GROUPS):
        each(complete, g)
    sent(all_sent, send_sem.at[0])


def write_out(in_ref, w_ref, gain_ref, shift_ref, bias_ref, out_hbm, wout_hbm, gain_hbm, shift_hbm, bias_hbm, sem):
    pairs = [(w_ref.at[a], wout_hbm.at[a]) for a in range(3)]
    pairs += [(in_ref, out_hbm), (gain_ref, gain_hbm), (shift_ref, shift_hbm), (bias_ref, bias_hbm)]
    copies = [pltpu.make_async_copy(src, to, sem.at[n]) for n, (src, to) in enumerate(pairs)]
    for copy in copies:
        copy.start()
    for copy in copies:
        copy.wait()


def body(activations, cotangent, conv_weight, norm_gain, norm_shift):
    anywhere = pl.BlockSpec(memory_space=pl.ANY)
    vmem = pl.BlockSpec(memory_space=pltpu.VMEM)
    dma = pltpu.SemaphoreType.DMA
    results = pl.pallas_call(
        kernel,
        out_shape=(
            pltpu.VMEM((NF, NR, W, C), BF16),
            pltpu.VMEM((3, 3, 3, C, C), F32),
            pltpu.VMEM((1, C), F32),
            pltpu.VMEM((1, C), F32),
            pltpu.VMEM((1, C), F32),
        ),
        in_specs=[anywhere] * 5,
        out_specs=(vmem,) * 5,
        scratch_shapes=[
            pltpu.VMEM((1, C), F32),
            pltpu.VMEM((1, C), F32),
            pltpu.VMEM((NF, NR, W, C), BF16),
            pltpu.VMEM((NF + 2, NR + 2, W, C), BF16),
            pltpu.VMEM((9, 3 * C, C), BF16),
            pltpu.VMEM((NF, NR, 3 * C, W), BF16),
            pltpu.VMEM((NF, NR, W, C), F32),
            pltpu.VMEM((NF, NR, W, C), F32),
            pltpu.VMEM((3, 9, C, C), F32),
            pltpu.VMEM((3, 9, 64, C), F32),
            pltpu.VMEM((3, 3, 4, 9, 16, C), F32),
            pltpu.VMEM((3, 9, C, C), BF16),
            pltpu.VMEM((2, 2, 4, C), F32),
            pltpu.VMEM((2, 16, 4, C), F32),
            pltpu.VMEM((2, 8, 4, C), F32),
            pltpu.VMEM((SENT, C), F32),
            dma((NF + 4,)), dma((5,)), dma((6,)), dma((3,)), dma((2, 2)), dma((3,)), dma((3, 3)),
            dma((GROUPS, 3)), dma((GROUPS, 3)), dma((GROUPS, 3)), dma((2, 3)),
        ],
        compiler_params=pltpu.CompilerParams(
            collective_id=0, has_side_effects=True, vmem_limit_bytes=64_100_000
        ),
    )(
        activations,
        cotangent,
        conv_weight.reshape(9, 3 * C, C),
        norm_gain.reshape(1, C),
        norm_shift.reshape(1, C),
    )
    per_channel = jax.ShapeDtypeStruct((1, C), F32)
    input_grad, weight_grad, gain_grad, shift_grad, bias_grad = pl.pallas_call(
        write_out,
        out_shape=(
            jax.ShapeDtypeStruct((NF, NR, W, C), BF16),
            jax.ShapeDtypeStruct((3, 3, 3, C, C), F32),
            per_channel,
            per_channel,
            per_channel,
        ),
        in_specs=[vmem] * 5,
        out_specs=(anywhere,) * 5,
        scratch_shapes=[dma((7,))],
        compiler_params=pltpu.CompilerParams(vmem_limit_bytes=16 * 1024 * 1024),
    )(*results)
    return input_grad, weight_grad, gain_grad.reshape(C), shift_grad.reshape(C), bias_grad.reshape(C)


def solution(mesh):
    placed = (P("span", "slab", None, None), P("span", "slab", None, None), P(), P(), P())
    return jax.shard_map(
        body,
        mesh=mesh,
        in_specs=placed,
        out_specs=(P("span", "slab", None, None), P(), P(), P(), P()),
        check_vma=False,
    )
```
